256 devices in a mesh: lon: 32 (over y_hi, z, core), lat: 8 (over x, y_lo).
Axes of the slice: x: 4, y: 4 (y_hi: 2, y_lo: 2; y = y_hi * 2 + y_lo), z: 8, core: 2. Of those that a mesh axis runs over, the one named last changes fastest.
Arguments:
- state: float32 [4, 32, 256, 4096], P(None, None, 'lat', 'lon'), may hold values from -6 to 6
- land_mask: int32 [256, 4096], P('lat', 'lon'), may hold values 0 or 1
- wet_levels: int32 [256, 4096], P('lat', 'lon'), may hold values from 1 to 32
Outputs:
- new_state: float32 [4, 32, 256, 4096], P(None, None, 'lat', 'lon')
The draws below stay inside these ranges and needn't reach their ends.
All inputs are finite; a program needn't handle non-finite values. No bound on the sum of `land_mask` on one device may be relied on, other than what follows from the above.
Results may differ from the reference program's by a relative error of at most 0.00002.
Values sent between devices are 32-bit elements; how exact they have to be, the bound alone decides.
A program may use at most 128 MiB of HBM per device.

```python
import jax
import jax.numpy as jnp
from jax import lax

LEV = 32
STEPS = 2
NY = 256
NX = 4096


def set_ends(entries, stream_key, smallest, top_value):
    longest = entries.shape.index(max(entries.shape))
    spots = []
    for shift in (0, 1):
        where = [jax.random.randint(jax.random.fold_in(stream_key, axis), (), 0, length) for axis, length in enumerate(entries.shape)]
        where[longest] = (where[longest] + shift) % entries.shape[longest]
        spots.append(tuple(where))
    return entries.at[spots[0]].set(smallest).at[spots[1]].set(top_value)


def shard_levels(own_key, extent, shards, low, high):
    level, own = 1.0, jax.random.fold_in(own_key, 6)
    for axis_at, blocks in shards:
        draws = jnp.exp(jax.random.uniform(jax.random.fold_in(own, axis_at), (blocks,), jnp.float32, low / len(shards), high / len(shards)))
        level = level * jnp.repeat(draws, extent[axis_at] // blocks).reshape([-1 if axis == axis_at else 1 for axis in range(len(extent))])
    return level


def gaussian(rng, dims, scale, limit, shards=(), held_as=jnp.bfloat16):
    entries = jax.random.normal(rng, dims, jnp.float32) * scale
    if len(shards) > 0:
        entries = shard_levels(rng, dims, shards, -0.22, 0.18) * entries
    return jnp.clip(entries, min=-limit, max=limit).astype(held_as)


def setup_inputs(seed: int = 0) -> dict:
    seeds = jax.random.split(jax.random.key(seed), 4)
    state = gaussian(seeds[0], (4, LEV, NY, NX), 1.0, 6.0, ((2, 8), (3, 32)), jnp.float32)
    land_mask = set_ends((jax.random.randint(seeds[1], (NY, NX), 0, 4) < 3).astype(jnp.int32), jax.random.fold_in(seeds[1], 1), 0, 1)
    wet_levels = set_ends(jax.random.randint(seeds[2], (NY, NX), 1, LEV + 1), jax.random.fold_in(seeds[2], 1), 1, LEV).astype(jnp.int32)
    return dict(state=state, land_mask=land_mask, wet_levels=wet_levels)


time_step = 0.1
lateral_mix = 0.5
column_mix = 0.5
gravity = 0.5
thermal = 0.2
haline = 0.8


def wetness(land_mask, wet_levels, levels):
    level_ids = jnp.arange(levels, dtype=jnp.int32)[:, None, None]
    return ((land_mask[None] == 1) & (level_ids < wet_levels[None])).astype(jnp.float32)


def pressure(extended):
    density = haline * extended[1] - thermal * extended[0]
    return gravity * (jnp.cumsum(density, axis=0) - 0.5 * density)


def explicit(state, east_west, north_south, press_ew, press_ns, coriolis, wet):
    grad_x = (8.0 * (east_west[..., 3:-1] - east_west[..., 1:-3]) - (east_west[..., 4:] - east_west[..., :-4])) / 12.0
    grad_y = (8.0 * (north_south[..., 3:-1, :] - north_south[..., 1:-3, :]) - (north_south[..., 4:, :] - north_south[..., :-4, :])) / 12.0
    spread = (east_west[..., 3:-1] + east_west[..., 1:-3]) + (north_south[..., 3:-1, :] + north_south[..., 1:-3, :]) - 4.0 * state
    east_vel = state[2]
    north_vel = state[3]
    carried = east_vel * grad_x + north_vel * grad_y
    press_x = 0.5 * (press_ew[..., 3:-1] - press_ew[..., 1:-3])
    press_y = 0.5 * (press_ns[..., 3:-1, :] - press_ns[..., 1:-3, :])
    zero = jnp.zeros_like(press_x)
    force = jnp.stack([zero, zero, coriolis * north_vel - press_x, -coriolis * east_vel - press_y])
    return (state + time_step * (lateral_mix * spread - carried + force)) * wet


def reference(state, land_mask, wet_levels):
    levels = state.shape[1]
    rows = state.shape[2]
    cols = state.shape[3]
    wet = wetness(land_mask, wet_levels, levels)
    coriolis = (0.2 + 0.8 * ((jnp.arange(rows, dtype=jnp.int32).astype(jnp.float32) + 0.5) / rows))[:, None]
    sign = jnp.array([1.0, 1.0, -1.0, -1.0], jnp.float32)[:, None, None, None]
    upper = jnp.concatenate([column_mix * wet[1:], jnp.zeros_like(wet[:1])], axis=0)
    lower = jnp.concatenate([jnp.zeros_like(wet[:1]), column_mix * wet[1:]], axis=0)
    centre = 1.0 + lower + upper
    current = state * wet
    for step in range(STEPS):
        east_west = jnp.concatenate([current[..., -2:], current, current[..., :2]], axis=3)
        fold = sign * current[:, :, -2:, ::-1][:, :, ::-1, :]
        north_south = jnp.concatenate([jnp.zeros_like(current[:, :, :2]), current, fold], axis=2)
        press_ew = pressure(east_west)
        press_ns = pressure(north_south)

        def one_level(level):
            return explicit(current[:, level], east_west[:, level], north_south[:, level],
                            press_ew[level], press_ns[level], coriolis, wet[level])

        levels_first = lax.map(one_level, jnp.arange(levels, dtype=jnp.int32))

        def forward(carry, inputs):
            ratio_prev, part_prev = carry
            rhs, low, high, middle = inputs
            denom = middle + low * ratio_prev
            ratio = -high / denom
            part = (rhs + low * part_prev) / denom
            return (ratio, part), (ratio, part)

        start = (jnp.zeros((rows, cols), jnp.float32), jnp.zeros((4, rows, cols), jnp.float32))
        unused, (ratios, parts) = lax.scan(forward, start, (levels_first, lower, upper, centre))

        def backward(below, inputs):
            ratio, part = inputs
            value = part - ratio * below
            return value, value

        unused_last, values = lax.scan(backward, jnp.zeros((4, rows, cols), jnp.float32), (ratios, parts), reverse=True)
        current = jnp.moveaxis(values, 0, 1)
    return current
```

```python
import functools

import jax
import jax.numpy as jnp
from jax import lax
from jax.experimental import pallas as pl
from jax.experimental.pallas import tpu as pltpu
from jax.sharding import PartitionSpec as P

MESH = pl.DeviceIdType.MESH
FIELDS, LEVELS, ROWS, COLS = 4, 32, 32, 128
TOP = 8
DEPTH = 48
GROUPS = ((0,), (1,), (2,), (3,))
INNER, OUTER = (1, 2), (0, 3)
SLOT = {1: 0, 2: 1, 0: 2, 3: 3}
UNROLL = 2


def factors():
    inside, last, ratio = [], [], 0.0
    for level in range(LEVELS):
        low = 0.5 if level > 0 else 0.0
        inside.append(0.5 / (1.5 + low + low * ratio))
        last.append(0.5 / (1.0 + low + low * ratio))
        ratio = -0.5 / (1.5 + low + low * ratio)
    return inside, last


def kernel(
    lons, lats, state_ref, land_ref, depth_ref, out_ref,
    cur, pivot, mask, send_lon, recv_lon, halo, result,
    load_sem, lat_send, lat_recv, lon_send, lon_recv, out_sem,
):
    lon, lat = lax.axis_index("lon"), lax.axis_index("lat")
    west = {"lon": lax.rem(lon + lons - 1, lons)}
    east = {"lon": lax.rem(lon + 1, lons)}
    north, south = {"lat": lat + 1}, {"lat": lat - 1}
    fold = {"lon": lons - 1 - lon}
    is_top, is_bottom = lat == lats - 1, lat == 0
    not_top, not_bottom = lat < lats - 1, lat > 0

    barrier = pltpu.get_barrier_semaphore()

    def greet(device):
        pl.semaphore_signal(barrier, inc=1, device_id=device, device_id_type=MESH)

    greet(west)
    greet(east)
    pl.when(not_top)(lambda: greet(north))
    pl.when(is_top)(lambda: greet(fold))
    pl.when(not_bottom)(lambda: greet(south))

    loads = [
        pltpu.make_async_copy(land_ref, mask.at[0], load_sem.at[4]),
        pltpu.make_async_copy(depth_ref, mask.at[1], load_sem.at[5]),
    ] + [
        pltpu.make_async_copy(
            state_ref.at[f], cur.at[0, f, :, pl.ds(TOP, ROWS)], load_sem.at[f]
        )
        for f in range(FIELDS)
    ]
    for load in loads:
        load.start()

    lane = lax.broadcasted_iota(jnp.int32, (8, COLS), 1)
    sublane = lax.broadcasted_iota(jnp.int32, (8, COLS), 0)
    low_pair = lax.rem(lane, 4) < 2
    group_lane = lane // 4
    lane_0, lane_1 = lane == 0, lane <= 1
    lane_127, lane_126 = lane == COLS - 1, lane >= COLS - 2

    def coriolis(tile):
        row = (lat * ROWS + tile * 8 + sublane).astype(jnp.float32)
        return 0.2 * (0.2 + 0.8 * ((row + 0.5) / (lats * ROWS)))

    @pl.when(is_bottom)
    def _():
        def clear(i, carry):
            for step in range(2):
                for f in range(FIELDS):
                    cur[step, f, i, pl.ds(TOP - 2, 2), :] = jnp.zeros((2, COLS), jnp.float32)
            return carry

        lax.fori_loop(0, LEVELS, clear, 0)

    loads[0].wait()
    loads[1].wait()
    inside, last = factors()
    wet_count = []
    for tile in range(4):
        rows = pl.ds(8 * tile, 8)
        count = jnp.where(mask[0, rows, :] == 1, mask[1, rows, :], 0)
        wet_count.append(count)
        for level in range(LEVELS):
            pivot[level, rows, :] = jnp.where(
                count > level + 1, inside[level], jnp.where(count == level + 1, last[level], 0.0)
            )

    def lat_copies(step, index):
        group = GROUPS[index]
        fields = pl.ds(group[0], len(group))

        def rows(start):
            return cur.at[step, fields, :, pl.ds(start, 2)]

        up = (rows(TOP + ROWS - 2), rows(TOP - 2))
        down = (rows(TOP), rows(TOP + ROWS))
        to_fold = (rows(TOP + ROWS - 2), rows(TOP + ROWS))

        def remote(pair, side, sem_side, device):
            return pltpu.make_async_remote_copy(
                src_ref=pair[0],
                dst_ref=pair[1],
                send_sem=lat_send.at[step, side, index],
                recv_sem=lat_recv.at[step, sem_side, index],
                device_id=device,
                device_id_type=MESH,
            )

        return remote(up, 0, 0, north), remote(to_fold, 0, 1, fold), remote(down, 1, 1, south)

    def send_lat(step, index):
        up, across, down = lat_copies(step, index)
        pl.when(not_top)(lambda: up.start())
        pl.when(is_top)(lambda: across.start())
        pl.when(not_bottom)(lambda: down.start())

    def wait_lat(step, index):
        up, across, down = lat_copies(step, index)
        down.wait_recv()
        pl.when(not_bottom)(lambda: up.wait_recv())

        @pl.when(is_top)
        def _():
            reverse = (COLS - 1) - lax.broadcasted_iota(jnp.int32, (2, COLS), 1)

            def turn(level, carry):
                for f in GROUPS[index]:
                    got = cur[step, f, level, pl.ds(TOP + ROWS, 2), :]
                    got = jnp.take_along_axis(got, reverse, axis=1)
                    sign = 1.0 if f < 2 else -1.0
                    cur[step, f, level, pl.ds(TOP + ROWS, 1), :] = sign * got[1:2]
                    cur[step, f, level, pl.ds(TOP + ROWS + 1, 1), :] = sign * got[0:1]
                return carry

            lax.fori_loop(0, LEVELS, turn, 0)

    parts = ((pl.ds(0, 2), pl.ds(0, 2)), (pl.ds(2, 2), pl.ds(0, 1)), (pl.ds(2, 2), pl.ds(1, 1)))

    def lon_copies(step, part):
        tiles, pairs = parts[part]

        def remote(side, device):
            return pltpu.make_async_remote_copy(
                src_ref=send_lon.at[step, side, tiles, pairs],
                dst_ref=recv_lon.at[step, side, tiles, pairs],
                send_sem=lon_send.at[step, side, part],
                recv_sem=lon_recv.at[step, side, part],
                device_id=device,
                device_id_type=MESH,
            )

        return remote(0, east), remote(1, west)

    def pack_lon(step, tile, pair, first, second):
        slot = SLOT[tile]
        send_lon[step, 0, slot, pair] = jnp.where(low_pair, first, pltpu.roll(second, 2, 1))
        send_lon[step, 1, slot, pair] = jnp.where(low_pair, pltpu.roll(first, COLS - 2, 1), second)

    def send_lon_part(step, part):
        for copy in lon_copies(step, part):
            copy.start()

    def wait_lon(step, part):
        for copy in lon_copies(step, part):
            copy.wait_recv()
        tiles = INNER if part == 0 else OUTER
        pairs = (0, 1) if part == 0 else (part - 1,)
        for tile in tiles:
            for pair in pairs:
                from_west = recv_lon[step, 0, SLOT[tile], pair]
                from_east = recv_lon[step, 1, SLOT[tile], pair]
                halo[2 * pair, tile] = jnp.where(low_pair, from_west, pltpu.roll(from_east, 2, 1))
                halo[2 * pair + 1, tile] = jnp.where(
                    low_pair, pltpu.roll(from_west, COLS - 2, 1), from_east
                )

    def collect(level, value, packed):
        return jnp.where(group_lane == level, pltpu.roll(value, 4 * level + 2, 1), packed)

    zero = jnp.zeros((8, COLS), jnp.float32)

    for load in loads[2:]:
        load.wait()
    first_packs = {}
    for tiles in (OUTER, INNER):
        def cover(level, packs):
            packs = list(packs)
            at = 0
            for tile in tiles:
                wet = wet_count[tile] > level
                for f in range(FIELDS):
                    rows = pl.ds(TOP + 8 * tile, 8)
                    value = jnp.where(wet, cur[0, f, level, rows, :], 0.0)
                    cur[0, f, level, rows, :] = value
                    packs[at] = collect(level, value, packs[at])
                    at += 1
            return tuple(packs)

        packs = lax.fori_loop(0, LEVELS, cover, (zero,) * (4 * len(tiles)))
        for i, tile in enumerate(tiles):
            for pair in range(2):
                pack_lon(0, tile, pair, packs[4 * i + 2 * pair], packs[4 * i + 2 * pair + 1])
        if tiles == OUTER:
            pl.when(is_bottom)(lambda: pl.semaphore_wait(barrier, 3))
            pl.when(not_bottom)(lambda: pl.semaphore_wait(barrier, 4))
            for index in range(len(GROUPS)):
                send_lat(0, index)
    for part in range(3):
        send_lon_part(0, part)

    def advance(step, tiles, fields):
        force_x, force_y = 2 in fields, 3 in fields
        coriolis_of = {tile: coriolis(tile) for tile in tiles}
        units = [(tile, f) for tile in tiles for f in fields]
        forces = [(tile, axis) for tile in tiles for axis, on in enumerate((force_x, force_y)) if on]

        def store(f, level, tile, value):
            if step == 0:
                cur[1, f, level, pl.ds(TOP + 8 * tile, 8), :] = value
            else:
                result[f, level, pl.ds(8 * tile, 8), :] = value

        def load(f, level, tile):
            if step == 0:
                return cur[1, f, level, pl.ds(TOP + 8 * tile, 8), :]
            return result[f, level, pl.ds(8 * tile, 8), :]

        def at(f, level, tile, shift):
            return cur[step, f, level, pl.ds(TOP + 8 * tile + shift, 8), :]

        def down(level, carry):
            parts_done = dict(zip(units, carry[0]))
            sums = dict(zip(forces, carry[1]))
            for tile in tiles:
                own = {}

                def value(f):
                    if f not in own:
                        own[f] = at(f, level, tile, 0)
                    return own[f]

                edges = {}

                def edge(f):
                    if f not in edges:
                        edges[f] = pltpu.roll(halo[f, tile], 126 - 4 * level, 1)
                    return edges[f]

                near = {}

                def beside(f):
                    if (f, 0) not in near:
                        near[f, 0] = (
                            pltpu.roll(jnp.where(lane_0, edge(f), value(f)), COLS - 1, 1),
                            pltpu.roll(jnp.where(lane_127, edge(f), value(f)), 1, 1),
                        )
                    return near[f, 0]

                def above(f):
                    if (f, 1) not in near:
                        near[f, 1] = (at(f, level, tile, 1), at(f, level, tile, -1))
                    return near[f, 1]

                speed_x = value(2) * (1.0 / 60.0)
                speed_y = value(3) * (1.0 / 60.0)
                speed_x8, speed_y8 = 8.0 * speed_x, 8.0 * speed_y
                to_east, to_west = 0.1 - speed_x8, 0.1 + speed_x8
                to_north, to_south = 0.1 - speed_y8, 0.1 + speed_y8
                pivots = pivot[level, pl.ds(8 * tile, 8), :]
                for f in fields:
                    east_1, west_1 = beside(f)
                    east_2 = pltpu.roll(jnp.where(lane_1, edge(f), value(f)), COLS - 2, 1)
                    west_2 = pltpu.roll(jnp.where(lane_126, edge(f), value(f)), 2, 1)
                    north_1, south_1 = above(f)
                    north_2, south_2 = at(f, level, tile, 2), at(f, level, tile, -2)
                    total = (
                        (1.6 * value(f) + (east_1 * to_east + west_1 * to_west))
                        + (east_2 - west_2) * speed_x
                    ) + (
                        (north_1 * to_north + south_1 * to_south)
                        + (north_2 - south_2) * speed_y
                    )
                    if f >= 2:
                        sides = beside if f == 2 else above
                        plus_t, minus_t = sides(0)
                        plus_s, minus_s = sides(1)
                        half = 0.02 * (plus_s - minus_s) - 0.005 * (plus_t - minus_t)
                        middle = sums[tile, f - 2] + half
                        sums[tile, f - 2] = middle + half
                        turned = coriolis_of[tile] * value(5 - f)
                        total = total + ((turned if f == 2 else -turned) - middle)
                    part = pivots * (total + parts_done[tile, f])
                    parts_done[tile, f] = part
                    store(f, level, tile, part)
            return tuple(parts_done[u] for u in units), tuple(sums[k] for k in forces)

        def down_some(i, carry):
            for j in range(UNROLL):
                carry = down(i * UNROLL + j, carry)
            return carry

        lax.fori_loop(0, LEVELS // UNROLL, down_some, ((zero,) * len(units), (zero,) * len(forces)))

        def up(level, carry):
            values, packs = list(carry[0]), list(carry[1])
            for at_unit, (tile, f) in enumerate(units):
                pivots = pivot[level, pl.ds(8 * tile, 8), :]
                value = load(f, level, tile) + pivots * values[at_unit]
                store(f, level, tile, value)
                values[at_unit] = value
                if step == 0:
                    packs[at_unit] = collect(level, value, packs[at_unit])
            return tuple(values), tuple(packs)

        def up_some(i, carry):
            for j in range(UNROLL):
                carry = up(LEVELS - 1 - (i * UNROLL + j), carry)
            return carry

        start = ((zero,) * len(units), (zero,) * (len(units) if step == 0 else 0))
        packs = lax.fori_loop(0, LEVELS // UNROLL, up_some, start)[1]
        return dict(zip(units, packs))

    outs = []

    def write(fields, start, count):
        copy = pltpu.make_async_copy(
            result.at[fields, :, pl.ds(start, count)],
            out_ref.at[fields, :, pl.ds(start, count)],
            out_sem.at[len(outs)],
        )
        copy.start()
        outs.append(copy)

    every = tuple(range(FIELDS))
    for step in range(2):
        wait_lon(step, 0)
        packs = advance(step, INNER, every)
        if step == 0:
            for tile in INNER:
                for pair in range(2):
                    pack_lon(1, tile, pair, packs[tile, 2 * pair], packs[tile, 2 * pair + 1])
            send_lon_part(1, 0)
        else:
            write(pl.ds(0, FIELDS), 8, 16)
        wait_lon(step, 1)
        wait_lon(step, 2)
        packs = {}
        for index, group in enumerate(GROUPS):
            wait_lat(step, index)
            packs.update(advance(step, OUTER, group))
            if step == 0:
                send_lat(1, index)
                for pair in range(2):
                    if group[-1] == 2 * pair + 1:
                        for tile in OUTER:
                            pack_lon(1, tile, pair, packs[tile, 2 * pair], packs[tile, 2 * pair + 1])
                        send_lon_part(1, 1 + pair)
            else:
                write(pl.ds(group[0], len(group)), 0, 8)
                write(pl.ds(group[0], len(group)), 24, 8)

    for step in range(2):
        for index in range(len(GROUPS)):
            up, across, down = lat_copies(step, index)
            up.wait_send()
            pl.when(not_bottom)(lambda: down.wait_send())
        for part in range(3):
            for copy in lon_copies(step, part):
                copy.wait_send()
    for copy in outs:
        copy.wait()


def per_device(lons, lats, state, land_mask, wet_levels):
    any_spec = pl.BlockSpec(memory_space=pl.ANY)
    groups = len(GROUPS)
    return pl.pallas_call(
        functools.partial(kernel, lons, lats),
        out_shape=jax.ShapeDtypeStruct(state.shape, jnp.float32),
        in_specs=[any_spec] * 3,
        out_specs=any_spec,
        scratch_shapes=[
            pltpu.VMEM((2, FIELDS, LEVELS, DEPTH, COLS), jnp.float32),
            pltpu.VMEM((LEVELS, ROWS, COLS), jnp.float32),
            pltpu.VMEM((2, ROWS, COLS), jnp.int32),
            pltpu.VMEM((2, 2, 4, 2, 8, COLS), jnp.float32),
            pltpu.VMEM((2, 2, 4, 2, 8, COLS), jnp.float32),
            pltpu.VMEM((FIELDS, 4, 8, COLS), jnp.float32),
            pltpu.VMEM((FIELDS, LEVELS, ROWS, COLS), jnp.float32),
            pltpu.SemaphoreType.DMA((6,)),
            pltpu.SemaphoreType.DMA((2, 2, groups)),
            pltpu.SemaphoreType.DMA((2, 2, groups)),
            pltpu.SemaphoreType.DMA((2, 2, 3)),
            pltpu.SemaphoreType.DMA((2, 2, 3)),
            pltpu.SemaphoreType.DMA((1 + 2 * groups,)),
        ],
        compiler_params=pltpu.CompilerParams(collective_id=0, has_side_effects=True),
        name="ocean_steps",
    )(state, land_mask, wet_levels)


def solution(mesh):
    placed = (P(None, None, "lat", "lon"), P("lat", "lon"), P("lat", "lon"))
    return jax.shard_map(
        functools.partial(per_device, mesh.shape["lon"], mesh.shape["lat"]),
        mesh=mesh,
        in_specs=placed,
        out_specs=P(None, None, "lat", "lon"),
        check_vma=False,
    )
```

```python
import functools

import jax
import jax.numpy as jnp
from jax import lax
from jax.experimental import pallas as pl
from jax.experimental.pallas import tpu as pltpu
from jax.sharding import PartitionSpec as P

MESH = pl.DeviceIdType.MESH
FIELDS, LEVELS, ROWS, COLS = 4, 32, 32, 128
TOP = 8
DEPTH = 48
GROUPS = ((0,), (1,), (2,), (3,))
INNER, OUTER = (1, 2), (0, 3)
SLOT = {1: 0, 2: 1, 0: 2, 3: 3}
COVER = 8
X_UNROLL, Y_UNROLL = 4, 8


def repeat(count, body, carry):
    return body(0, carry) if count == 1 else lax.fori_loop(0, count, body, carry)


def factors():
    inside, last, ratio = [], [], 0.0
    for level in range(LEVELS):
        low = 0.5 if level > 0 else 0.0
        inside.append(0.5 / (1.5 + low + low * ratio))
        last.append(0.5 / (1.0 + low + low * ratio))
        ratio = -0.5 / (1.5 + low + low * ratio)
    return inside, last


def kernel(
    lons, lats, state_ref, land_ref, depth_ref, out_ref,
    cur, pivot, mask, send_lon, recv_lon, halo, edges, result,
    load_sem, lat_send, lat_recv, lon_send, lon_recv, out_sem,
):
    lon, lat = lax.axis_index("lon"), lax.axis_index("lat")
    west = {"lon": lax.rem(lon + lons - 1, lons)}
    east = {"lon": lax.rem(lon + 1, lons)}
    north, south = {"lat": lat + 1}, {"lat": lat - 1}
    fold = {"lon": lons - 1 - lon}
    is_top, is_bottom = lat == lats - 1, lat == 0
    not_top, not_bottom = lat < lats - 1, lat > 0

    barrier = pltpu.get_barrier_semaphore()

    def greet(device):
        pl.semaphore_signal(barrier, inc=1, device_id=device, device_id_type=MESH)

    greet(west)
    greet(east)
    pl.when(not_top)(lambda: greet(north))
    pl.when(is_top)(lambda: greet(fold))
    pl.when(not_bottom)(lambda: greet(south))

    loads = [
        pltpu.make_async_copy(land_ref, mask.at[0], load_sem.at[4]),
        pltpu.make_async_copy(depth_ref, mask.at[1], load_sem.at[5]),
    ] + [
        pltpu.make_async_copy(
            state_ref.at[f], cur.at[0, f, :, pl.ds(TOP, ROWS)], load_sem.at[f]
        )
        for f in range(FIELDS)
    ]
    for load in loads:
        load.start()

    lane = lax.broadcasted_iota(jnp.int32, (8, COLS), 1)
    sublane = lax.broadcasted_iota(jnp.int32, (8, COLS), 0)
    low_pair = lax.rem(lane, 4) < 2
    group_lane = lane // 4
    lane_0, lane_1 = lane == 0, lane <= 1
    lane_127, lane_126 = lane == COLS - 1, lane >= COLS - 2

    def coriolis(tile):
        row = (lat * ROWS + tile * 8 + sublane).astype(jnp.float32)
        return 0.2 * (0.2 + 0.8 * ((row + 0.5) / (lats * ROWS)))

    @pl.when(is_bottom)
    def _():
        def clear(i, carry):
            for step in range(2):
                for f in range(FIELDS):
                    cur[step, f, i, pl.ds(TOP - 2, 2), :] = jnp.zeros((2, COLS), jnp.float32)
            return carry

        lax.fori_loop(0, LEVELS, clear, 0)

    loads[0].wait()
    loads[1].wait()
    inside, last = factors()
    wet_count = []
    for tile in range(4):
        rows = pl.ds(8 * tile, 8)
        count = jnp.where(mask[0, rows, :] == 1, mask[1, rows, :], 0)
        wet_count.append(count)
        for level in range(LEVELS):
            pivot[level, rows, :] = jnp.where(
                count > level + 1, inside[level], jnp.where(count == level + 1, last[level], 0.0)
            )

    def lat_copies(step, index):
        group = GROUPS[index]
        fields = pl.ds(group[0], len(group))

        def rows(start):
            return cur.at[step, fields, :, pl.ds(start, 2)]

        up = (rows(TOP + ROWS - 2), rows(TOP - 2))
        down = (rows(TOP), rows(TOP + ROWS))
        to_fold = (rows(TOP + ROWS - 2), rows(TOP + ROWS))

        def remote(pair, side, sem_side, device):
            return pltpu.make_async_remote_copy(
                src_ref=pair[0],
                dst_ref=pair[1],
                send_sem=lat_send.at[step, side, index],
                recv_sem=lat_recv.at[step, sem_side, index],
                device_id=device,
                device_id_type=MESH,
            )

        return remote(up, 0, 0, north), remote(to_fold, 0, 1, fold), remote(down, 1, 1, south)

    def send_lat(step, index):
        up, across, down = lat_copies(step, index)
        pl.when(not_top)(lambda: up.start())
        pl.when(is_top)(lambda: across.start())
        pl.when(not_bottom)(lambda: down.start())

    def wait_lat(step, index):
        up, across, down = lat_copies(step, index)
        down.wait_recv()
        pl.when(not_bottom)(lambda: up.wait_recv())

        @pl.when(is_top)
        def _():
            reverse = (COLS - 1) - lax.broadcasted_iota(jnp.int32, (2, COLS), 1)

            for level in range(LEVELS):
                for f in GROUPS[index]:
                    got = cur[step, f, level, pl.ds(TOP + ROWS, 2), :]
                    got = jnp.take_along_axis(got, reverse, axis=1)
                    sign = 1.0 if f < 2 else -1.0
                    cur[step, f, level, pl.ds(TOP + ROWS, 1), :] = sign * got[1:2]
                    cur[step, f, level, pl.ds(TOP + ROWS + 1, 1), :] = sign * got[0:1]

    parts = ((pl.ds(0, 2), pl.ds(0, 2)), (pl.ds(2, 2), pl.ds(0, 1)), (pl.ds(2, 2), pl.ds(1, 1)))

    def lon_copies(step, part):
        tiles, pairs = parts[part]

        def remote(side, device):
            return pltpu.make_async_remote_copy(
                src_ref=send_lon.at[step, side, tiles, pairs],
                dst_ref=recv_lon.at[step, side, tiles, pairs],
                send_sem=lon_send.at[step, side, part],
                recv_sem=lon_recv.at[step, side, part],
                device_id=device,
                device_id_type=MESH,
            )

        return remote(0, east), remote(1, west)

    def pack_lon(step, tile, pair, first, second):
        slot = SLOT[tile]
        send_lon[step, 0, slot, pair] = jnp.where(low_pair, first, pltpu.roll(second, 2, 1))
        send_lon[step, 1, slot, pair] = jnp.where(low_pair, pltpu.roll(first, COLS - 2, 1), second)

    def send_lon_part(step, part):
        for copy in lon_copies(step, part):
            copy.start()

    def wait_lon(step, part):
        for copy in lon_copies(step, part):
            copy.wait_recv()
        tiles = INNER if part == 0 else OUTER
        pairs = (0, 1) if part == 0 else (part - 1,)
        for tile in tiles:
            for pair in pairs:
                from_west = recv_lon[step, 0, SLOT[tile], pair]
                from_east = recv_lon[step, 1, SLOT[tile], pair]
                halo[2 * pair, tile] = jnp.where(low_pair, from_west, pltpu.roll(from_east, 2, 1))
                halo[2 * pair + 1, tile] = jnp.where(
                    low_pair, pltpu.roll(from_west, COLS - 2, 1), from_east
                )

    def collect(place, value, packed):
        return jnp.where(group_lane == place, pltpu.roll(value, 4 * place + 2, 1), packed)

    def turn_lanes(value, amount):
        amount = amount % COLS
        return value if amount == 0 else pltpu.roll(value, amount, 1)

    zero = jnp.zeros((8, COLS), jnp.float32)

    for load in loads[2:]:
        load.wait()
    first_packs = {}
    for tiles in (OUTER, INNER):
        def cover(i, packs):
            packs = list(packs)
            for place in range(COVER):
                level = i * COVER + place
                at = 0
                for tile in tiles:
                    wet = wet_count[tile] > level
                    for f in range(FIELDS):
                        rows = pl.ds(TOP + 8 * tile, 8)
                        value = jnp.where(wet, cur[0, f, level, rows, :], 0.0)
                        cur[0, f, level, rows, :] = value
                        packs[at] = collect(place, value, packs[at])
                        at += 1
            return tuple(turn_lanes(pack, -4 * COVER) for pack in packs)

        packs = repeat(LEVELS // COVER, cover, (zero,) * (4 * len(tiles)))
        for i, tile in enumerate(tiles):
            for pair in range(2):
                pack_lon(0, tile, pair, packs[4 * i + 2 * pair], packs[4 * i + 2 * pair + 1])
        if tiles == OUTER:
            pl.when(is_bottom)(lambda: pl.semaphore_wait(barrier, 3))
            pl.when(not_bottom)(lambda: pl.semaphore_wait(barrier, 4))
            for index in range(len(GROUPS)):
                send_lat(0, index)
    for part in range(3):
        send_lon_part(0, part)

    def grow(step, f, level, tile):
        if step == 0:
            return cur.at[1, f, level, pl.ds(TOP + 8 * tile, 8), :]
        return result.at[f, level, pl.ds(8 * tile, 8), :]

    def at(step, f, level, tile, shift=0):
        return cur[step, f, level, pl.ds(TOP + 8 * tile + shift, 8), :]

    def spread_edges(tiles, fields):
        for tile in tiles:
            for f in fields:
                packed = halo[f, tile]
                for level in range(LEVELS):
                    edges[f, level, pl.ds(8 * tile, 8), :] = turn_lanes(packed, 126 - 4 * level)

    def sweep(step, tiles, fields, axis, last, unroll):
        units = [(tile, f) for tile in tiles for f in fields]
        forces = [tile for tile in tiles if 2 + axis in fields]
        turned = {tile: coriolis(tile) for tile in tiles} if axis == 0 else None

        def one(level, parts_done, sums):
            for tile in tiles:
                near = {}

                def value(f):
                    if (f, 0) not in near:
                        near[f, 0] = at(step, f, level, tile)
                    return near[f, 0]

                def edge(f):
                    if (f, 1) not in near:
                        near[f, 1] = edges[f, level, pl.ds(8 * tile, 8), :]
                    return near[f, 1]

                def sides(f):
                    if (f, 2) not in near:
                        if axis == 0:
                            near[f, 2] = (
                                pltpu.roll(jnp.where(lane_0, edge(f), value(f)), COLS - 1, 1),
                                pltpu.roll(jnp.where(lane_127, edge(f), value(f)), 1, 1),
                            )
                        else:
                            near[f, 2] = at(step, f, level, tile, 1), at(step, f, level, tile, -1)
                    return near[f, 2]

                def far_sides(f):
                    if axis == 0:
                        return (
                            pltpu.roll(jnp.where(lane_1, edge(f), value(f)), COLS - 2, 1),
                            pltpu.roll(jnp.where(lane_126, edge(f), value(f)), 2, 1),
                        )
                    return at(step, f, level, tile, 2), at(step, f, level, tile, -2)

                speed = value(2 + axis) * (1.0 / 60.0)
                speed_8 = 8.0 * speed
                to_plus, to_minus = 0.1 - speed_8, 0.1 + speed_8
                for f in fields:
                    plus, minus = sides(f)
                    plus_2, minus_2 = far_sides(f)
                    total = (plus * to_plus + minus * to_minus) + (plus_2 - minus_2) * speed
                    if axis == 0:
                        total = total + 1.6 * value(f)
                        if f == 2:
                            total = total + turned[tile] * value(3)
                        if f == 3:
                            total = total - turned[tile] * value(2)
                    if f == 2 + axis:
                        plus_t, minus_t = sides(0)
                        plus_s, minus_s = sides(1)
                        half = 0.02 * (plus_s - minus_s) - 0.005 * (plus_t - minus_t)
                        middle = sums[tile] + half
                        sums[tile] = middle + half
                        total = total - middle
                    ref = grow(step, f, level, tile)
                    if last:
                        pivots = pivot[level, pl.ds(8 * tile, 8), :]
                        total = pivots * ((total + ref[...]) + parts_done[tile, f])
                        parts_done[tile, f] = total
                    ref[...] = total

        def some(i, carry):
            parts_done = dict(zip(units, carry[0]))
            sums = dict(zip(forces, carry[1]))
            for place in range(unroll):
                one(i * unroll + place, parts_done, sums)
            return tuple(parts_done[u] for u in units) if last else (), tuple(sums[k] for k in forces)

        start = ((zero,) * len(units) if last else (), (zero,) * len(forces))
        repeat(LEVELS // unroll, some, start)

    def substitute(step, tiles, fields, unroll):
        units = [(tile, f) for tile in tiles for f in fields]
        trips = LEVELS // unroll

        def some(i, carry):
            values, packs = list(carry[0]), [turn_lanes(pack, 4 * unroll) for pack in carry[1]]
            for place in reversed(range(unroll)):
                level = (trips - 1 - i) * unroll + place
                for at_unit, (tile, f) in enumerate(units):
                    ref = grow(step, f, level, tile)
                    value = ref[...] + pivot[level, pl.ds(8 * tile, 8), :] * values[at_unit]
                    ref[...] = value
                    values[at_unit] = value
                    if step == 0:
                        packs[at_unit] = collect(place, value, packs[at_unit])
            return tuple(values), tuple(packs)

        start = ((zero,) * len(units), (zero,) * (len(units) if step == 0 else 0))
        return dict(zip(units, repeat(trips, some, start)[1]))

    outs = []

    def write(fields, start, count):
        copy = pltpu.make_async_copy(
            result.at[fields, :, pl.ds(start, count)],
            out_ref.at[fields, :, pl.ds(start, count)],
            out_sem.at[len(outs)],
        )
        copy.start()
        outs.append(copy)

    every = tuple(range(FIELDS))

    def pack_next(tiles, pair, packs):
        for tile in tiles:
            pack_lon(1, tile, pair, packs[tile, 2 * pair], packs[tile, 2 * pair + 1])

    sweep(0, INNER, every, 1, False, 2)
    for part in range(3):
        wait_lon(0, part)
    spread_edges(OUTER, every)
    sweep(0, OUTER, every, 0, False, X_UNROLL)
    spread_edges(INNER, every)
    sweep(0, INNER, every, 0, True, X_UNROLL)
    packs = substitute(0, INNER, every, 8)
    for pair in range(2):
        pack_next(INNER, pair, packs)
    send_lon_part(1, 0)
    packs = {}
    for index, group in enumerate(GROUPS):
        wait_lat(0, index)
        sweep(0, OUTER, group, 1, True, Y_UNROLL)
        packs.update(substitute(0, OUTER, group, 16))
        send_lat(1, index)
        for pair in range(2):
            if group[-1] == 2 * pair + 1:
                pack_next(OUTER, pair, packs)
                send_lon_part(1, 1 + pair)

    sweep(1, INNER, every, 1, False, 2)
    wait_lon(1, 0)
    spread_edges(INNER, every)
    sweep(1, INNER, every, 0, True, X_UNROLL)
    substitute(1, INNER, every, 8)
    write(pl.ds(0, FIELDS), 8, 16)
    for part in (1, 2):
        wait_lon(1, part)
    spread_edges(OUTER, every)
    sweep(1, OUTER, every, 0, False, X_UNROLL)
    for index, group in enumerate(GROUPS):
        wait_lat(1, index)
        sweep(1, OUTER, group, 1, True, Y_UNROLL)
        substitute(1, OUTER, group, 16)
        write(pl.ds(group[0], len(group)), 0, 8)
        write(pl.ds(group[0], len(group)), 24, 8)

    for step in range(2):
        for index in range(len(GROUPS)):
            up, across, down = lat_copies(step, index)
            up.wait_send()
            pl.when(not_bottom)(lambda: down.wait_send())
        for part in range(3):
            for copy in lon_copies(step, part):
                copy.wait_send()
    for copy in outs:
        copy.wait()


def per_device(lons, lats, state, land_mask, wet_levels):
    any_spec = pl.BlockSpec(memory_space=pl.ANY)
    groups = len(GROUPS)
    return pl.pallas_call(
        functools.partial(kernel, lons, lats),
        out_shape=jax.ShapeDtypeStruct(state.shape, jnp.float32),
        in_specs=[any_spec] * 3,
        out_specs=any_spec,
        scratch_shapes=[
            pltpu.VMEM((2, FIELDS, LEVELS, DEPTH, COLS), jnp.float32),
            pltpu.VMEM((LEVELS, ROWS, COLS), jnp.float32),
            pltpu.VMEM((2, ROWS, COLS), jnp.int32),
            pltpu.VMEM((2, 2, 4, 2, 8, COLS), jnp.float32),
            pltpu.VMEM((2, 2, 4, 2, 8, COLS), jnp.float32),
            pltpu.VMEM((FIELDS, 4, 8, COLS), jnp.float32),
            pltpu.VMEM((FIELDS, LEVELS, ROWS, COLS), jnp.float32),
            pltpu.VMEM((FIELDS, LEVELS, ROWS, COLS), jnp.float32),
            pltpu.SemaphoreType.DMA((6,)),
            pltpu.SemaphoreType.DMA((2, 2, groups)),
            pltpu.SemaphoreType.DMA((2, 2, groups)),
            pltpu.SemaphoreType.DMA((2, 2, 3)),
            pltpu.SemaphoreType.DMA((2, 2, 3)),
            pltpu.SemaphoreType.DMA((1 + 2 * groups,)),
        ],
        compiler_params=pltpu.CompilerParams(collective_id=0, has_side_effects=True),
        name="ocean_steps",
    )(state, land_mask, wet_levels)


def solution(mesh):
    placed = (P(None, None, "lat", "lon"), P("lat", "lon"), P("lat", "lon"))
    return jax.shard_map(
        functools.partial(per_device, mesh.shape["lon"], mesh.shape["lat"]),
        mesh=mesh,
        in_specs=placed,
        out_specs=P(None, None, "lat", "lon"),
        check_vma=False,
    )
```

```python
import functools

import jax
import jax.numpy as jnp
from jax import lax
from jax.experimental import pallas as pl
from jax.experimental.pallas import tpu as pltpu
from jax.sharding import PartitionSpec as P

MESH = pl.DeviceIdType.MESH
FIELDS, LEVELS, ROWS, COLS = 4, 32, 32, 128
TOP = 8
DEPTH = 48
GROUPS = ((0,), (1,), (2,), (3,))
INNER, OUTER = (1, 2), (0, 3)
SLOT = {1: 0, 2: 1, 0: 2, 3: 3}
COVER = 8
X_UNROLL, Y_UNROLL = 4, 8


def repeat(count, body, carry):
    return body(0, carry) if count == 1 else lax.fori_loop(0, count, body, carry)


def factors():
    inside, last, ratio = [], [], 0.0
    for level in range(LEVELS):
        low = 0.5 if level > 0 else 0.0
        inside.append(0.5 / (1.5 + low + low * ratio))
        last.append(0.5 / (1.0 + low + low * ratio))
        ratio = -0.5 / (1.5 + low + low * ratio)
    return inside, last


def kernel(
    lons, lats, state_ref, land_ref, depth_ref, result,
    cur, pivot, mask, send_lon, recv_lon, halo, edges,
    load_sem, lat_send, lat_recv, lon_send, lon_recv,
):
    lon, lat = lax.axis_index("lon"), lax.axis_index("lat")
    west = {"lon": lax.rem(lon + lons - 1, lons)}
    east = {"lon": lax.rem(lon + 1, lons)}
    north, south = {"lat": lat + 1}, {"lat": lat - 1}
    fold = {"lon": lons - 1 - lon}
    is_top, is_bottom = lat == lats - 1, lat == 0
    not_top, not_bottom = lat < lats - 1, lat > 0

    barrier = pltpu.get_barrier_semaphore()

    def greet(device):
        pl.semaphore_signal(barrier, inc=1, device_id=device, device_id_type=MESH)

    greet(west)
    greet(east)
    pl.when(not_top)(lambda: greet(north))
    pl.when(is_top)(lambda: greet(fold))
    pl.when(not_bottom)(lambda: greet(south))

    loads = [
        pltpu.make_async_copy(land_ref, mask.at[0], load_sem.at[4]),
        pltpu.make_async_copy(depth_ref, mask.at[1], load_sem.at[5]),
    ] + [
        pltpu.make_async_copy(
            state_ref.at[f], cur.at[0, f, :, pl.ds(TOP, ROWS)], load_sem.at[f]
        )
        for f in range(FIELDS)
    ]
    for load in loads:
        load.start()

    lane = lax.broadcasted_iota(jnp.int32, (8, COLS), 1)
    sublane = lax.broadcasted_iota(jnp.int32, (8, COLS), 0)
    low_pair = lax.rem(lane, 4) < 2
    group_lane = lane // 4
    lane_0, lane_1 = lane == 0, lane <= 1
    lane_127, lane_126 = lane == COLS - 1, lane >= COLS - 2

    def coriolis(tile):
        row = (lat * ROWS + tile * 8 + sublane).astype(jnp.float32)
        return 0.2 * (0.2 + 0.8 * ((row + 0.5) / (lats * ROWS)))

    @pl.when(is_bottom)
    def _():
        def clear(i, carry):
            for step in range(2):
                for f in range(FIELDS):
                    cur[step, f, i, pl.ds(TOP - 2, 2), :] = jnp.zeros((2, COLS), jnp.float32)
            return carry

        lax.fori_loop(0, LEVELS, clear, 0)

    loads[0].wait()
    loads[1].wait()
    inside, last = factors()
    wet_count = []
    for tile in range(4):
        rows = pl.ds(8 * tile, 8)
        count = jnp.where(mask[0, rows, :] == 1, mask[1, rows, :], 0)
        wet_count.append(count)
        for level in range(LEVELS):
            pivot[level, rows, :] = jnp.where(
                count > level + 1, inside[level], jnp.where(count == level + 1, last[level], 0.0)
            )

    def lat_copies(step, index):
        group = GROUPS[index]
        fields = pl.ds(group[0], len(group))

        def rows(start):
            return cur.at[step, fields, :, pl.ds(start, 2)]

        up = (rows(TOP + ROWS - 2), rows(TOP - 2))
        down = (rows(TOP), rows(TOP + ROWS))
        to_fold = (rows(TOP + ROWS - 2), rows(TOP + ROWS))

        def remote(pair, side, sem_side, device):
            return pltpu.make_async_remote_copy(
                src_ref=pair[0],
                dst_ref=pair[1],
                send_sem=lat_send.at[step, side, index],
                recv_sem=lat_recv.at[step, sem_side, index],
                device_id=device,
                device_id_type=MESH,
            )

        return remote(up, 0, 0, north), remote(to_fold, 0, 1, fold), remote(down, 1, 1, south)

    def send_lat(step, index):
        up, across, down = lat_copies(step, index)
        pl.when(not_top)(lambda: up.start())
        pl.when(is_top)(lambda: across.start())
        pl.when(not_bottom)(lambda: down.start())

    def wait_lat(step, index):
        up, across, down = lat_copies(step, index)
        down.wait_recv()
        pl.when(not_bottom)(lambda: up.wait_recv())

        @pl.when(is_top)
        def _():
            reverse = (COLS - 1) - lax.broadcasted_iota(jnp.int32, (2, COLS), 1)

            for level in range(LEVELS):
                for f in GROUPS[index]:
                    got = cur[step, f, level, pl.ds(TOP + ROWS, 2), :]
                    got = jnp.take_along_axis(got, reverse, axis=1)
                    sign = 1.0 if f < 2 else -1.0
                    cur[step, f, level, pl.ds(TOP + ROWS, 1), :] = sign * got[1:2]
                    cur[step, f, level, pl.ds(TOP + ROWS + 1, 1), :] = sign * got[0:1]

    parts = ((pl.ds(0, 2), pl.ds(0, 2)), (pl.ds(2, 2), pl.ds(0, 1)), (pl.ds(2, 2), pl.ds(1, 1)))

    def lon_copies(step, part):
        tiles, pairs = parts[part]

        def remote(side, device):
            return pltpu.make_async_remote_copy(
                src_ref=send_lon.at[step, side, tiles, pairs],
                dst_ref=recv_lon.at[step, side, tiles, pairs],
                send_sem=lon_send.at[step, side, part],
                recv_sem=lon_recv.at[step, side, part],
                device_id=device,
                device_id_type=MESH,
            )

        return remote(0, east), remote(1, west)

    def pack_lon(step, tile, pair, first, second):
        slot = SLOT[tile]
        send_lon[step, 0, slot, pair] = jnp.where(low_pair, first, pltpu.roll(second, 2, 1))
        send_lon[step, 1, slot, pair] = jnp.where(low_pair, pltpu.roll(first, COLS - 2, 1), second)

    def send_lon_part(step, part):
        for copy in lon_copies(step, part):
            copy.start()

    def wait_lon(step, part):
        for copy in lon_copies(step, part):
            copy.wait_recv()
        tiles = INNER if part == 0 else OUTER
        pairs = (0, 1) if part == 0 else (part - 1,)
        for tile in tiles:
            for pair in pairs:
                from_west = recv_lon[step, 0, SLOT[tile], pair]
                from_east = recv_lon[step, 1, SLOT[tile], pair]
                halo[2 * pair, tile] = jnp.where(low_pair, from_west, pltpu.roll(from_east, 2, 1))
                halo[2 * pair + 1, tile] = jnp.where(
                    low_pair, pltpu.roll(from_west, COLS - 2, 1), from_east
                )

    def collect(place, value, packed):
        return jnp.where(group_lane == place, pltpu.roll(value, 4 * place + 2, 1), packed)

    def turn_lanes(value, amount):
        amount = amount % COLS
        return value if amount == 0 else pltpu.roll(value, amount, 1)

    zero = jnp.zeros((8, COLS), jnp.float32)

    for load in loads[2:]:
        load.wait()
    first_packs = {}
    for tiles in (OUTER, INNER):
        def cover(i, packs):
            packs = list(packs)
            for place in range(COVER):
                level = i * COVER + place
                at = 0
                for tile in tiles:
                    wet = wet_count[tile] > level
                    for f in range(FIELDS):
                        rows = pl.ds(TOP + 8 * tile, 8)
                        value = jnp.where(wet, cur[0, f, level, rows, :], 0.0)
                        cur[0, f, level, rows, :] = value
                        packs[at] = collect(place, value, packs[at])
                        at += 1
            return tuple(turn_lanes(pack, -4 * COVER) for pack in packs)

        packs = repeat(LEVELS // COVER, cover, (zero,) * (4 * len(tiles)))
        for i, tile in enumerate(tiles):
            for pair in range(2):
                pack_lon(0, tile, pair, packs[4 * i + 2 * pair], packs[4 * i + 2 * pair + 1])
        if tiles == OUTER:
            pl.when(is_bottom)(lambda: pl.semaphore_wait(barrier, 3))
            pl.when(not_bottom)(lambda: pl.semaphore_wait(barrier, 4))
            for index in range(len(GROUPS)):
                send_lat(0, index)
    for part in range(3):
        send_lon_part(0, part)

    def grow(step, f, level, tile):
        if step == 0:
            return cur.at[1, f, level, pl.ds(TOP + 8 * tile, 8), :]
        return result.at[f, level, pl.ds(8 * tile, 8), :]

    def at(step, f, level, tile, shift=0):
        return cur[step, f, level, pl.ds(TOP + 8 * tile + shift, 8), :]

    def spread_edges(tiles, fields):
        for tile in tiles:
            for f in fields:
                packed = halo[f, tile]
                for level in range(LEVELS):
                    edges[f, level, pl.ds(8 * tile, 8), :] = turn_lanes(packed, 126 - 4 * level)

    def sweep(step, tiles, fields, axis, last, unroll):
        units = [(tile, f) for tile in tiles for f in fields]
        forces = [tile for tile in tiles if 2 + axis in fields]
        turned = {tile: coriolis(tile) for tile in tiles} if axis == 0 else None

        def one(level, parts_done, sums):
            for tile in tiles:
                near = {}

                def value(f):
                    if (f, 0) not in near:
                        near[f, 0] = at(step, f, level, tile)
                    return near[f, 0]

                def edge(f):
                    if (f, 1) not in near:
                        near[f, 1] = edges[f, level, pl.ds(8 * tile, 8), :]
                    return near[f, 1]

                def sides(f):
                    if (f, 2) not in near:
                        if axis == 0:
                            near[f, 2] = (
                                pltpu.roll(jnp.where(lane_0, edge(f), value(f)), COLS - 1, 1),
                                pltpu.roll(jnp.where(lane_127, edge(f), value(f)), 1, 1),
                            )
                        else:
                            near[f, 2] = at(step, f, level, tile, 1), at(step, f, level, tile, -1)
                    return near[f, 2]

                def far_sides(f):
                    if axis == 0:
                        return (
                            pltpu.roll(jnp.where(lane_1, edge(f), value(f)), COLS - 2, 1),
                            pltpu.roll(jnp.where(lane_126, edge(f), value(f)), 2, 1),
                        )
                    return at(step, f, level, tile, 2), at(step, f, level, tile, -2)

                speed = value(2 + axis) * (1.0 / 60.0)
                speed_8 = 8.0 * speed
                to_plus, to_minus = 0.1 - speed_8, 0.1 + speed_8
                for f in fields:
                    plus, minus = sides(f)
                    plus_2, minus_2 = far_sides(f)
                    total = (plus * to_plus + minus * to_minus) + (plus_2 - minus_2) * speed
                    if axis == 0:
                        total = total + 1.6 * value(f)
                        if f == 2:
                            total = total + turned[tile] * value(3)
                        if f == 3:
                            total = total - turned[tile] * value(2)
                    if f == 2 + axis:
                        plus_t, minus_t = sides(0)
                        plus_s, minus_s = sides(1)
                        half = 0.02 * (plus_s - minus_s) - 0.005 * (plus_t - minus_t)
                        middle = sums[tile] + half
                        sums[tile] = middle + half
                        total = total - middle
                    ref = grow(step, f, level, tile)
                    if last:
                        pivots = pivot[level, pl.ds(8 * tile, 8), :]
                        total = pivots * ((total + ref[...]) + parts_done[tile, f])
                        parts_done[tile, f] = total
                    ref[...] = total

        def some(i, carry):
            parts_done = dict(zip(units, carry[0]))
            sums = dict(zip(forces, carry[1]))
            for place in range(unroll):
                one(i * unroll + place, parts_done, sums)
            return tuple(parts_done[u] for u in units) if last else (), tuple(sums[k] for k in forces)

        start = ((zero,) * len(units) if last else (), (zero,) * len(forces))
        repeat(LEVELS // unroll, some, start)

    def substitute(step, tiles, fields, unroll):
        units = [(tile, f) for tile in tiles for f in fields]
        trips = LEVELS // unroll

        def some(i, carry):
            values, packs = list(carry[0]), [turn_lanes(pack, 4 * unroll) for pack in carry[1]]
            for place in reversed(range(unroll)):
                level = (trips - 1 - i) * unroll + place
                for at_unit, (tile, f) in enumerate(units):
                    ref = grow(step, f, level, tile)
                    value = ref[...] + pivot[level, pl.ds(8 * tile, 8), :] * values[at_unit]
                    ref[...] = value
                    values[at_unit] = value
                    if step == 0:
                        packs[at_unit] = collect(place, value, packs[at_unit])
            return tuple(values), tuple(packs)

        start = ((zero,) * len(units), (zero,) * (len(units) if step == 0 else 0))
        return dict(zip(units, repeat(trips, some, start)[1]))

    every = tuple(range(FIELDS))

    def pack_next(tiles, pair, packs):
        for tile in tiles:
            pack_lon(1, tile, pair, packs[tile, 2 * pair], packs[tile, 2 * pair + 1])

    sweep(0, INNER, every, 1, False, 2)
    for part in range(3):
        wait_lon(0, part)
    spread_edges(OUTER, every)
    sweep(0, OUTER, every, 0, False, X_UNROLL)
    spread_edges(INNER, every)
    sweep(0, INNER, every, 0, True, X_UNROLL)
    packs = substitute(0, INNER, every, 8)
    for pair in range(2):
        pack_next(INNER, pair, packs)
    send_lon_part(1, 0)
    packs = {}
    for index, group in enumerate(GROUPS):
        wait_lat(0, index)
        sweep(0, OUTER, group, 1, True, Y_UNROLL)
        packs.update(substitute(0, OUTER, group, 16))
        send_lat(1, index)
        for pair in range(2):
            if group[-1] == 2 * pair + 1:
                pack_next(OUTER, pair, packs)
                send_lon_part(1, 1 + pair)

    sweep(1, INNER, every, 1, False, 2)
    wait_lon(1, 0)
    spread_edges(INNER, every)
    sweep(1, INNER, every, 0, True, X_UNROLL)
    substitute(1, INNER, every, 8)
    for part in (1, 2):
        wait_lon(1, part)
    spread_edges(OUTER, every)
    sweep(1, OUTER, every, 0, False, X_UNROLL)
    for index, group in enumerate(GROUPS):
        wait_lat(1, index)
        sweep(1, OUTER, group, 1, True, Y_UNROLL)
        substitute(1, OUTER, group, 16)

    for step in range(2):
        for index in range(len(GROUPS)):
            up, across, down = lat_copies(step, index)
            up.wait_send()
            pl.when(not_bottom)(lambda: down.wait_send())
        for part in range(3):
            for copy in lon_copies(step, part):
                copy.wait_send()


def per_device(lons, lats, state, land_mask, wet_levels):
    any_spec = pl.BlockSpec(memory_space=pl.ANY)
    groups = len(GROUPS)
    return pl.pallas_call(
        functools.partial(kernel, lons, lats),
        out_shape=jax.ShapeDtypeStruct(state.shape, jnp.float32),
        in_specs=[pl.BlockSpec(memory_space=pltpu.HBM)] * 3,
        out_specs=pl.BlockSpec(memory_space=pltpu.VMEM),
        scratch_shapes=[
            pltpu.VMEM((2, FIELDS, LEVELS, DEPTH, COLS), jnp.float32),
            pltpu.VMEM((LEVELS, ROWS, COLS), jnp.float32),
            pltpu.VMEM((2, ROWS, COLS), jnp.int32),
            pltpu.VMEM((2, 2, 4, 2, 8, COLS), jnp.float32),
            pltpu.VMEM((2, 2, 4, 2, 8, COLS), jnp.float32),
            pltpu.VMEM((FIELDS, 4, 8, COLS), jnp.float32),
            pltpu.VMEM((FIELDS, LEVELS, ROWS, COLS), jnp.float32),
            pltpu.SemaphoreType.DMA((6,)),
            pltpu.SemaphoreType.DMA((2, 2, groups)),
            pltpu.SemaphoreType.DMA((2, 2, groups)),
            pltpu.SemaphoreType.DMA((2, 2, 3)),
            pltpu.SemaphoreType.DMA((2, 2, 3)),
        ],
        compiler_params=pltpu.CompilerParams(collective_id=0, has_side_effects=True, vmem_limit_bytes=24 * 2**20),
        name="ocean_steps",
    )(*(pltpu.with_memory_space_constraint(x, pltpu.HBM) for x in (state, land_mask, wet_levels)))


def solution(mesh):
    placed = (P(None, None, "lat", "lon"), P("lat", "lon"), P("lat", "lon"))
    return jax.shard_map(
        functools.partial(per_device, mesh.shape["lon"], mesh.shape["lat"]),
        mesh=mesh,
        in_specs=placed,
        out_specs=P(None, None, "lat", "lon"),
        check_vma=False,
    )
```

```python
import functools

import jax
import jax.numpy as jnp
from jax import lax
from jax.experimental import pallas as pl
from jax.experimental.pallas import tpu as pltpu
from jax.sharding import PartitionSpec as P

MESH = pl.DeviceIdType.MESH
FIELDS, LEVELS, ROWS, COLS = 4, 32, 32, 128
TOP = 8
DEPTH = 48
GROUPS = ((0,), (1,), (2,), (3,))
INNER, OUTER = (1, 2), (0, 3)
SLOT = {1: 0, 2: 1, 0: 2, 3: 3}
COVER = 8
X_LEVELS, Y_UNROLL = 32, 8


def repeat(count, body, carry):
    return body(0, carry) if count == 1 else lax.fori_loop(0, count, body, carry)


def factors():
    inside, last, ratio = [], [], 0.0
    for level in range(LEVELS):
        low = 0.5 if level > 0 else 0.0
        inside.append(0.5 / (1.5 + low + low * ratio))
        last.append(0.5 / (1.0 + low + low * ratio))
        ratio = -0.5 / (1.5 + low + low * ratio)
    return inside, last


def kernel(
    lons, lats, state_ref, land_ref, depth_ref, result,
    cur, pivot, mask, send_lon, recv_lon, halo, edges, relayed, own, filters,
    load_sem, lat_send, lat_recv, lon_send, lon_recv,
):
    lon, lat = lax.axis_index("lon"), lax.axis_index("lat")
    west = {"lon": lax.rem(lon + lons - 1, lons)}
    east = {"lon": lax.rem(lon + 1, lons)}
    north, south = {"lat": lat + 1}, {"lat": lat - 1}
    relay = {"lon": lons - 1 - lon, "lat": lat - 1}
    origin = {"lon": lons - 1 - lon, "lat": lat + 1}
    is_top, is_bottom = lat == lats - 1, lat == 0
    not_top, not_bottom = lat < lats - 1, lat > 0
    is_relay = lat == lats - 2

    barrier = pltpu.get_barrier_semaphore()

    def greet(device):
        pl.semaphore_signal(barrier, inc=1, device_id=device, device_id_type=MESH)

    greet(west)
    greet(east)
    pl.when(not_top)(lambda: greet(north))
    pl.when(is_top)(lambda: greet(relay))
    pl.when(is_relay)(lambda: greet(origin))
    pl.when(not_bottom)(lambda: greet(south))

    loads = [
        pltpu.make_async_copy(land_ref, mask.at[0], load_sem.at[4]),
        pltpu.make_async_copy(depth_ref, mask.at[1], load_sem.at[5]),
    ] + [
        pltpu.make_async_copy(
            state_ref.at[f], cur.at[0, f, :, pl.ds(TOP, ROWS)], load_sem.at[f]
        )
        for f in range(FIELDS)
    ]
    for load in loads:
        load.start()

    lane = lax.broadcasted_iota(jnp.int32, (8, COLS), 1)
    sublane = lax.broadcasted_iota(jnp.int32, (8, COLS), 0)
    quarter = lax.rem(lane, 4)
    low_pair = quarter < 2
    group_lane = lane // 4

    source = lax.broadcasted_iota(jnp.int32, (COLS, COLS), 0)
    offset = lax.rem(source - lax.broadcasted_iota(jnp.int32, (COLS, COLS), 1) + COLS, COLS)

    def weigh(plus, minus, plus_2, minus_2):
        weights = jnp.where(offset == 1, plus, jnp.where(offset == COLS - 1, minus, 0.0))
        weights = jnp.where(offset == 2, plus_2, jnp.where(offset == COLS - 2, minus_2, weights))
        return weights.astype(jnp.bfloat16)

    for at_filter, taps in enumerate(((1.0, 1.0, 0.0, 0.0), (8.0, -8.0, -1.0, 1.0), (1.0, -1.0, 0.0, 0.0))):
        weights = weigh(*taps)
        for half in range(2):
            filters[pl.ds(COLS * half, COLS), pl.ds(COLS * at_filter, COLS)] = weights

    def coriolis(tile):
        row = (lat * ROWS + tile * 8 + sublane).astype(jnp.float32)
        return 0.2 * (0.2 + 0.8 * ((row + 0.5) / (lats * ROWS)))

    @pl.when(is_bottom)
    def _():
        def clear(i, carry):
            for step in range(2):
                for f in range(FIELDS):
                    cur[step, f, i, pl.ds(TOP - 2, 2), :] = jnp.zeros((2, COLS), jnp.float32)
            return carry

        lax.fori_loop(0, LEVELS, clear, 0)

    loads[0].wait()
    loads[1].wait()
    inside, last = factors()
    wet_count = []
    for tile in range(4):
        rows = pl.ds(8 * tile, 8)
        count = jnp.where(mask[0, rows, :] == 1, mask[1, rows, :], 0)
        wet_count.append(count)
        for level in range(LEVELS):
            pivot[level, rows, :] = jnp.where(
                count > level + 1, inside[level], jnp.where(count == level + 1, last[level], 0.0)
            )

    def lat_copies(step, index):
        group = GROUPS[index]
        fields = pl.ds(group[0], len(group))

        def rows(start):
            return cur.at[step, fields, :, pl.ds(start, 2)]

        up = (rows(TOP + ROWS - 2), rows(TOP - 2))
        down = (rows(TOP), rows(TOP + ROWS))
        held = relayed.at[step, fields, :, pl.ds(0, 2)]
        across = (rows(TOP + ROWS - 2), held)
        onward = (held, rows(TOP + ROWS))

        def remote(pair, send_sem, recv_sem, device):
            return pltpu.make_async_remote_copy(
                src_ref=pair[0],
                dst_ref=pair[1],
                send_sem=send_sem.at[step, index],
                recv_sem=recv_sem.at[step, index],
                device_id=device,
                device_id_type=MESH,
            )

        return (
            remote(up, lat_send.at[0], lat_recv.at[0], north),
            remote(across, lat_send.at[0], lat_recv.at[2], relay),
            remote(down, lat_send.at[1], lat_recv.at[1], south),
            remote(onward, lat_send.at[2], lat_recv.at[1], north),
        )

    def send_lat(step, index):
        up, across, down, _ = lat_copies(step, index)
        pl.when(not_top)(lambda: up.start())
        pl.when(is_top)(lambda: across.start())
        pl.when(not_bottom)(lambda: down.start())

    def hand_on(step, index):
        _, across, _, onward = lat_copies(step, index)

        @pl.when(is_relay)
        def _():
            across.wait_recv()
            onward.start()

    def wait_lat(step, index):
        up, _, down, _ = lat_copies(step, index)
        down.wait_recv()
        pl.when(not_bottom)(lambda: up.wait_recv())

        @pl.when(is_top)
        def _():
            reverse = (COLS - 1) - lax.broadcasted_iota(jnp.int32, (2, COLS), 1)

            for level in range(LEVELS):
                for f in GROUPS[index]:
                    got = cur[step, f, level, pl.ds(TOP + ROWS, 2), :]
                    got = jnp.take_along_axis(got, reverse, axis=1)
                    sign = 1.0 if f < 2 else -1.0
                    cur[step, f, level, pl.ds(TOP + ROWS, 1), :] = sign * got[1:2]
                    cur[step, f, level, pl.ds(TOP + ROWS + 1, 1), :] = sign * got[0:1]

    parts = ((pl.ds(0, 2), pl.ds(0, 2)), (pl.ds(2, 2), pl.ds(0, 1)), (pl.ds(2, 2), pl.ds(1, 1)))

    def lon_copies(step, part):
        tiles, pairs = parts[part]

        def remote(side, device):
            return pltpu.make_async_remote_copy(
                src_ref=send_lon.at[step, side, tiles, pairs],
                dst_ref=recv_lon.at[step, side, tiles, pairs],
                send_sem=lon_send.at[step, side, part],
                recv_sem=lon_recv.at[step, side, part],
                device_id=device,
                device_id_type=MESH,
            )

        return remote(0, east), remote(1, west)

    def pack_lon(step, tile, pair, first, second):
        slot = SLOT[tile]
        own[step, 2 * pair, tile] = first
        own[step, 2 * pair + 1, tile] = second
        send_lon[step, 0, slot, pair] = jnp.where(low_pair, first, pltpu.roll(second, 2, 1))
        send_lon[step, 1, slot, pair] = jnp.where(low_pair, pltpu.roll(first, COLS - 2, 1), second)

    def send_lon_part(step, part):
        for copy in lon_copies(step, part):
            copy.start()

    def wait_lon(step, part):
        for copy in lon_copies(step, part):
            copy.wait_recv()
        tiles = INNER if part == 0 else OUTER
        pairs = (0, 1) if part == 0 else (part - 1,)
        for tile in tiles:
            for pair in pairs:
                from_west = recv_lon[step, 0, SLOT[tile], pair]
                from_east = recv_lon[step, 1, SLOT[tile], pair]
                halo[2 * pair, tile] = jnp.where(low_pair, from_west, pltpu.roll(from_east, 2, 1))
                halo[2 * pair + 1, tile] = jnp.where(
                    low_pair, pltpu.roll(from_west, COLS - 2, 1), from_east
                )

    def collect(place, value, packed):
        return jnp.where(group_lane == place, pltpu.roll(value, 4 * place + 2, 1), packed)

    def turn_lanes(value, amount):
        amount = amount % COLS
        return value if amount == 0 else pltpu.roll(value, amount, 1)

    zero = jnp.zeros((8, COLS), jnp.float32)

    for load in loads[2:]:
        load.wait()
    first_packs = {}
    for tiles in (OUTER, INNER):
        def cover(i, packs):
            packs = list(packs)
            for place in range(COVER):
                level = i * COVER + place
                at = 0
                for tile in tiles:
                    wet = wet_count[tile] > level
                    for f in range(FIELDS):
                        rows = pl.ds(TOP + 8 * tile, 8)
                        value = jnp.where(wet, cur[0, f, level, rows, :], 0.0)
                        cur[0, f, level, rows, :] = value
                        packs[at] = collect(place, value, packs[at])
                        at += 1
            return tuple(turn_lanes(pack, -4 * COVER) for pack in packs)

        packs = repeat(LEVELS // COVER, cover, (zero,) * (4 * len(tiles)))
        for i, tile in enumerate(tiles):
            for pair in range(2):
                pack_lon(0, tile, pair, packs[4 * i + 2 * pair], packs[4 * i + 2 * pair + 1])
        if tiles == OUTER:
            pl.when(is_bottom)(lambda: pl.semaphore_wait(barrier, 3))
            pl.when(not_bottom & (lat != lats - 2))(lambda: pl.semaphore_wait(barrier, 4))
            pl.when(is_relay)(lambda: pl.semaphore_wait(barrier, 5))
            for index in range(len(GROUPS)):
                send_lat(0, index)
    for part in range(3):
        send_lon_part(0, part)

    def grow(step, f, level, tile):
        if step == 0:
            return cur.at[1, f, level, pl.ds(TOP + 8 * tile, 8), :]
        return result.at[f, level, pl.ds(8 * tile, 8), :]

    def at(step, f, level, tile, shift=0):
        return cur[step, f, level, pl.ds(TOP + 8 * tile + shift, 8), :]

    def split(value):
        high = value.astype(jnp.bfloat16)
        low = (value - high.astype(jnp.float32)).astype(jnp.bfloat16)
        return jnp.concatenate([high, low], axis=1)

    def along(step, tiles):
        flat = (8 * X_LEVELS, COLS)
        for tile in tiles:
            rows = pl.ds(TOP + 8 * tile, 8)
            turned = jnp.broadcast_to(coriolis(tile)[None], (X_LEVELS, 8, COLS)).reshape(flat)

            def some(i, total):
                levels = pl.ds(i * X_LEVELS, X_LEVELS)
                value = [cur[step, f, levels, rows, :].reshape(flat) for f in range(FIELDS)]
                mixed = jnp.dot(
                    jnp.concatenate([split(v) for v in value], axis=0),
                    filters[:, : 2 * COLS],
                    preferred_element_type=jnp.float32,
                )
                half = jnp.dot(
                    split(0.02 * value[1] - 0.005 * value[0]),
                    filters[:, 2 * COLS :],
                    preferred_element_type=jnp.float32,
                )
                middles = []
                for place in range(X_LEVELS):
                    part = half[8 * place : 8 * place + 8]
                    middles.append(total + part)
                    total = middles[-1] + part
                speed = value[2] * (1.0 / 60.0)
                for f in range(FIELDS):
                    both = mixed[flat[0] * f : flat[0] * (f + 1)]
                    grown = (1.6 * value[f] + 0.1 * both[:, :COLS]) - speed * both[:, COLS:]
                    if f == 2:
                        grown = grown + (turned * value[3] - jnp.concatenate(middles, axis=0))
                    if f == 3:
                        grown = grown - turned * value[2]
                    grown = grown.reshape(X_LEVELS, 8, COLS)
                    if step == 0:
                        cur[1, f, levels, rows, :] = grown
                    else:
                        result[f, levels, pl.ds(8 * tile, 8), :] = grown
                return total

            lax.fori_loop(0, LEVELS // X_LEVELS, some, zero)

    def repair(step, tiles):
        at_126, at_127, at_0 = quarter == 0, quarter == 1, quarter == 2
        at_edge = (lane < 2) | (lane >= COLS - 2)
        for tile in tiles:
            speed = own[step, 2, tile] * (1.0 / 60.0)
            gap = [halo[f, tile] - own[step, f, tile] for f in range(FIELDS)]
            change = []
            for f in range(FIELDS):
                back_1, on_1 = pltpu.roll(gap[f], COLS - 1, 1), pltpu.roll(gap[f], 1, 1)
                back_2, on_2 = pltpu.roll(gap[f], COLS - 2, 1), pltpu.roll(gap[f], 2, 1)
                near = jnp.where(at_127, back_1, jnp.where(at_0, on_1, 0.0))
                far = jnp.where(
                    at_126,
                    -back_2,
                    jnp.where(at_127, 8.0 * back_1 - back_2, jnp.where(at_0, on_2 - 8.0 * on_1, on_2)),
                )
                change.append(0.1 * near - speed * far)
            dense = 0.02 * gap[1] - 0.005 * gap[0]
            half = jnp.where(
                at_127, pltpu.roll(dense, COLS - 1, 1), jnp.where(at_0, -pltpu.roll(dense, 1, 1), 0.0)
            )
            total = half
            for shift in (4, 8, 16, 32, 64):
                total = total + jnp.where(lane >= shift, pltpu.roll(total, shift, 1), 0.0)
            change[2] = change[2] - (2.0 * total - half)
            for f in range(FIELDS):
                for level in range(LEVELS):
                    edges[f, level, pl.ds(8 * tile, 8), :] = jnp.where(
                        at_edge, turn_lanes(change[f], 126 - 4 * level), 0.0
                    )

    def sweep(step, tiles, fields, unroll):
        units = [(tile, f) for tile in tiles for f in fields]
        forces = [tile for tile in tiles if 3 in fields]

        def one(level, parts_done, sums):
            for tile in tiles:
                sides = {}

                def beside(f):
                    if f not in sides:
                        sides[f] = at(step, f, level, tile, 1), at(step, f, level, tile, -1)
                    return sides[f]

                speed = at(step, 3, level, tile) * (1.0 / 60.0)
                speed_8 = 8.0 * speed
                to_plus, to_minus = 0.1 - speed_8, 0.1 + speed_8
                pivots = pivot[level, pl.ds(8 * tile, 8), :]
                for f in fields:
                    plus, minus = beside(f)
                    gap = at(step, f, level, tile, 2) - at(step, f, level, tile, -2)
                    total = (plus * to_plus + minus * to_minus) + gap * speed
                    if f == 3:
                        plus_t, minus_t = beside(0)
                        plus_s, minus_s = beside(1)
                        half = 0.02 * (plus_s - minus_s) - 0.005 * (plus_t - minus_t)
                        middle = sums[tile] + half
                        sums[tile] = middle + half
                        total = total - middle
                    ref = grow(step, f, level, tile)
                    known = ref[...] + edges[f, level, pl.ds(8 * tile, 8), :]
                    total = pivots * ((total + known) + parts_done[tile, f])
                    parts_done[tile, f] = total
                    ref[...] = total

        def some(i, carry):
            parts_done = dict(zip(units, carry[0]))
            sums = dict(zip(forces, carry[1]))
            for place in range(unroll):
                one(i * unroll + place, parts_done, sums)
            return tuple(parts_done[u] for u in units), tuple(sums[k] for k in forces)

        repeat(LEVELS // unroll, some, ((zero,) * len(units), (zero,) * len(forces)))

    def substitute(step, tiles, fields, unroll):
        units = [(tile, f) for tile in tiles for f in fields]
        trips = LEVELS // unroll

        def some(i, carry):
            values, packs = list(carry[0]), [turn_lanes(pack, 4 * unroll) for pack in carry[1]]
            for place in reversed(range(unroll)):
                level = (trips - 1 - i) * unroll + place
                for at_unit, (tile, f) in enumerate(units):
                    ref = grow(step, f, level, tile)
                    value = ref[...] + pivot[level, pl.ds(8 * tile, 8), :] * values[at_unit]
                    ref[...] = value
                    values[at_unit] = value
                    if step == 0:
                        packs[at_unit] = collect(place, value, packs[at_unit])
            return tuple(values), tuple(packs)

        start = ((zero,) * len(units), (zero,) * (len(units) if step == 0 else 0))
        return dict(zip(units, repeat(trips, some, start)[1]))

    every = tuple(range(FIELDS))

    def pack_next(tiles, pair, packs):
        for tile in tiles:
            pack_lon(1, tile, pair, packs[tile, 2 * pair], packs[tile, 2 * pair + 1])

    along(0, OUTER)
    along(0, INNER)
    for part in range(3):
        wait_lon(0, part)
    repair(0, OUTER)
    hand_on(0, 0)
    repair(0, INNER)
    sweep(0, INNER, every, 2)
    hand_on(0, 1)
    packs = substitute(0, INNER, every, 8)
    for pair in range(2):
        pack_next(INNER, pair, packs)
    send_lon_part(1, 0)
    hand_on(0, 2)
    packs = {}
    for index, group in enumerate(GROUPS):
        wait_lat(0, index)
        if index == 1:
            hand_on(0, 3)
        sweep(0, OUTER, group, Y_UNROLL)
        packs.update(substitute(0, OUTER, group, 16))
        send_lat(1, index)
        for pair in range(2):
            if group[-1] == 2 * pair + 1:
                pack_next(OUTER, pair, packs)
                send_lon_part(1, 1 + pair)

    along(1, INNER)
    wait_lon(1, 0)
    repair(1, INNER)
    sweep(1, INNER, every, 2)
    substitute(1, INNER, every, 8)
    along(1, OUTER)
    for part in (1, 2):
        wait_lon(1, part)
    repair(1, OUTER)
    for index, group in enumerate(GROUPS):
        wait_lat(1, index)
        hand_on(1, index)
        sweep(1, OUTER, group, Y_UNROLL)
        substitute(1, OUTER, group, 16)

    for step in range(2):
        for index in range(len(GROUPS)):
            up, _, down, onward = lat_copies(step, index)
            up.wait_send()
            pl.when(not_bottom)(lambda: down.wait_send())
            pl.when(is_relay)(lambda: onward.wait_send())
        for part in range(3):
            for copy in lon_copies(step, part):
                copy.wait_send()


def per_device(lons, lats, state, land_mask, wet_levels):
    any_spec = pl.BlockSpec(memory_space=pl.ANY)
    groups = len(GROUPS)
    return pl.pallas_call(
        functools.partial(kernel, lons, lats),
        out_shape=jax.ShapeDtypeStruct(state.shape, jnp.float32),
        in_specs=[pl.BlockSpec(memory_space=pltpu.HBM)] * 3,
        out_specs=pl.BlockSpec(memory_space=pltpu.VMEM),
        scratch_shapes=[
            pltpu.VMEM((2, FIELDS, LEVELS, DEPTH, COLS), jnp.float32),
            pltpu.VMEM((LEVELS, ROWS, COLS), jnp.float32),
            pltpu.VMEM((2, ROWS, COLS), jnp.int32),
            pltpu.VMEM((2, 2, 4, 2, 8, COLS), jnp.float32),
            pltpu.VMEM((2, 2, 4, 2, 8, COLS), jnp.float32),
            pltpu.VMEM((FIELDS, 4, 8, COLS), jnp.float32),
            pltpu.VMEM((FIELDS, LEVELS, ROWS, COLS), jnp.float32),
            pltpu.VMEM((2, FIELDS, LEVELS, 8, COLS), jnp.float32),
            pltpu.VMEM((2, FIELDS, 4, 8, COLS), jnp.float32),
            pltpu.VMEM((2 * COLS, 3 * COLS), jnp.bfloat16),
            pltpu.SemaphoreType.DMA((6,)),
            pltpu.SemaphoreType.DMA((3, 2, groups)),
            pltpu.SemaphoreType.DMA((3, 2, groups)),
            pltpu.SemaphoreType.DMA((2, 2, 3)),
            pltpu.SemaphoreType.DMA((2, 2, 3)),
        ],
        compiler_params=pltpu.CompilerParams(collective_id=0, has_side_effects=True, vmem_limit_bytes=24 * 2**20),
        name="ocean_steps",
    )(*(pltpu.with_memory_space_constraint(x, pltpu.HBM) for x in (state, land_mask, wet_levels)))


def solution(mesh):
    placed = (P(None, None, "lat", "lon"), P("lat", "lon"), P("lat", "lon"))
    return jax.shard_map(
        functools.partial(per_device, mesh.shape["lon"], mesh.shape["lat"]),
        mesh=mesh,
        in_specs=placed,
        out_specs=P(None, None, "lat", "lon"),
        check_vma=False,
    )
```

```python
import functools

import jax
import jax.numpy as jnp
from jax import lax
from jax.experimental import pallas as pl
from jax.experimental.pallas import tpu as pltpu
from jax.sharding import PartitionSpec as P

MESH = pl.DeviceIdType.MESH
FIELDS, LEVELS, ROWS, COLS = 4, 32, 32, 128
TOP = 8
DEPTH = 48
GROUPS = ((0, 1), (2, 3))
INNER, OUTER = (1, 2), (0, 3)
SLOT = {1: 0, 2: 1, 0: 2, 3: 3}
COVER = 8
X_LEVELS, Y_UNROLL = 32, 8


def repeat(count, body, carry):
    return body(0, carry) if count == 1 else lax.fori_loop(0, count, body, carry)


def factors():
    inside, last, ratio = [], [], 0.0
    for level in range(LEVELS):
        low = 0.5 if level > 0 else 0.0
        inside.append(0.5 / (1.5 + low + low * ratio))
        last.append(0.5 / (1.0 + low + low * ratio))
        ratio = -0.5 / (1.5 + low + low * ratio)
    return inside, last


def kernel(
    lons, lats, state_ref, land_ref, depth_ref, result,
    cur, pivot, mask, send_lon, recv_lon, halo, edges, own, filters,
    load_sem, lat_send, lat_recv, lon_send, lon_recv,
):
    lon, lat = lax.axis_index("lon"), lax.axis_index("lat")
    west = {"lon": lax.rem(lon + lons - 1, lons)}
    east = {"lon": lax.rem(lon + 1, lons)}
    north, south = {"lat": lat + 1}, {"lat": lat - 1}
    fold = {"lon": lons - 1 - lon}
    is_top, is_bottom = lat == lats - 1, lat == 0
    not_top, not_bottom = lat < lats - 1, lat > 0

    barrier = pltpu.get_barrier_semaphore()

    def greet(device):
        pl.semaphore_signal(barrier, inc=1, device_id=device, device_id_type=MESH)

    greet(west)
    greet(east)
    pl.when(not_top)(lambda: greet(north))
    pl.when(is_top)(lambda: greet(fold))
    pl.when(not_bottom)(lambda: greet(south))

    loads = [
        pltpu.make_async_copy(land_ref, mask.at[0], load_sem.at[3]),
        pltpu.make_async_copy(depth_ref, mask.at[1], load_sem.at[4]),
    ] + [
        pltpu.make_async_copy(
            state_ref.at[:, :, pl.ds(8 * first, 8 * count)],
            cur.at[0, :, :, pl.ds(TOP + 8 * first, 8 * count)],
            load_sem.at[at_load],
        )
        for at_load, (first, count) in enumerate(((0, 1), (3, 1), (1, 2)))
    ]
    for load in loads:
        load.start()

    lane = lax.broadcasted_iota(jnp.int32, (8, COLS), 1)
    sublane = lax.broadcasted_iota(jnp.int32, (8, COLS), 0)
    quarter = lax.rem(lane, 4)
    low_pair = quarter < 2
    group_lane = lane // 4

    def coriolis(tile):
        row = (lat * ROWS + tile * 8 + sublane).astype(jnp.float32)
        return 0.2 * (0.2 + 0.8 * ((row + 0.5) / (lats * ROWS)))

    @pl.when(is_bottom)
    def _():
        def clear(i, carry):
            for step in range(2):
                for f in range(FIELDS):
                    cur[step, f, i, pl.ds(TOP - 2, 2), :] = jnp.zeros((2, COLS), jnp.float32)
            return carry

        lax.fori_loop(0, LEVELS, clear, 0)

    def lat_copies(step, index):
        group = GROUPS[index]
        fields = pl.ds(group[0], len(group))

        def rows(start):
            return cur.at[step, fields, :, pl.ds(start, 2)]

        up = (rows(TOP + ROWS - 2), rows(TOP - 2))
        down = (rows(TOP), rows(TOP + ROWS))
        across = (rows(TOP + ROWS - 2), rows(TOP + ROWS))

        def remote(pair, send_sem, recv_sem, device):
            return pltpu.make_async_remote_copy(
                src_ref=pair[0],
                dst_ref=pair[1],
                send_sem=send_sem.at[step, index],
                recv_sem=recv_sem.at[step, index],
                device_id=device,
                device_id_type=MESH,
            )

        return (
            remote(up, lat_send.at[0], lat_recv.at[0], north),
            remote(across, lat_send.at[0], lat_recv.at[1], fold),
            remote(down, lat_send.at[1], lat_recv.at[1], south),
        )

    def send_up(step, index):
        up, across, _ = lat_copies(step, index)
        pl.when(not_top)(lambda: up.start())
        pl.when(is_top)(lambda: across.start())

    def send_down(step, index):
        down = lat_copies(step, index)[2]
        pl.when(not_bottom)(lambda: down.start())

    def wait_below(step, index):
        up = lat_copies(step, index)[0]
        pl.when(not_bottom)(lambda: up.wait_recv())

    def wait_above(step, index):
        lat_copies(step, index)[2].wait_recv()

        @pl.when(is_top)
        def _():
            reverse = (COLS - 1) - lane
            flat = cur.reshape(2, FIELDS, LEVELS * DEPTH, COLS)
            for f in GROUPS[index]:
                for first in range(0, LEVELS, 8):
                    places = [pl.ds(first * DEPTH + TOP + ROWS + m, 8, stride=DEPTH) for m in range(2)]
                    got = [flat[step, f, place, :] for place in places]
                    got = [jnp.take_along_axis(value, reverse, axis=1) for value in got]
                    if f >= 2:
                        got = [-value for value in got]
                    flat[step, f, places[0], :] = got[1]
                    flat[step, f, places[1], :] = got[0]

    parts = ((pl.ds(0, 2), INNER), (pl.ds(2, 1), (0,)), (pl.ds(3, 1), (3,)))

    def lon_copies(step, part):
        slots = parts[part][0]

        def remote(side, device):
            return pltpu.make_async_remote_copy(
                src_ref=send_lon.at[step, side, slots],
                dst_ref=recv_lon.at[step, side, slots],
                send_sem=lon_send.at[step, side, part],
                recv_sem=lon_recv.at[step, side, part],
                device_id=device,
                device_id_type=MESH,
            )

        return remote(0, east), remote(1, west)

    def pack_lon(step, tile, pair, first, second):
        slot = SLOT[tile]
        own[step, 2 * pair, tile] = first
        own[step, 2 * pair + 1, tile] = second
        send_lon[step, 0, slot, pair] = jnp.where(low_pair, first, pltpu.roll(second, 2, 1))
        send_lon[step, 1, slot, pair] = jnp.where(low_pair, pltpu.roll(first, COLS - 2, 1), second)

    def send_lon_part(step, part):
        for copy in lon_copies(step, part):
            copy.start()

    def wait_lon(step, part):
        for copy in lon_copies(step, part):
            copy.wait_recv()
        for tile in parts[part][1]:
            for pair in range(2):
                from_west = recv_lon[step, 0, SLOT[tile], pair]
                from_east = recv_lon[step, 1, SLOT[tile], pair]
                halo[2 * pair, tile] = jnp.where(low_pair, from_west, pltpu.roll(from_east, 2, 1))
                halo[2 * pair + 1, tile] = jnp.where(
                    low_pair, pltpu.roll(from_west, COLS - 2, 1), from_east
                )

    def collect(place, value, packed):
        return jnp.where(group_lane == place, pltpu.roll(value, 4 * place + 2, 1), packed)

    def turn_lanes(value, amount):
        amount = amount % COLS
        return value if amount == 0 else pltpu.roll(value, amount, 1)

    zero = jnp.zeros((8, COLS), jnp.float32)

    loads[0].wait()
    loads[1].wait()
    wet_count = [
        jnp.where(mask[0, pl.ds(8 * tile, 8), :] == 1, mask[1, pl.ds(8 * tile, 8), :], 0)
        for tile in range(4)
    ]

    def cover(tiles):
        def some(i, carry):
            for place in range(COVER):
                level = i * COVER + place
                for tile in tiles:
                    wet = wet_count[tile] > level
                    for f in range(FIELDS):
                        rows = pl.ds(TOP + 8 * tile, 8)
                        cur[0, f, level, rows, :] = jnp.where(wet, cur[0, f, level, rows, :], 0.0)
            return carry

        lax.fori_loop(0, LEVELS // COVER, some, 0)

    def pack_first(tiles):
        units = [(tile, f) for tile in tiles for f in range(FIELDS)]

        def some(i, packs):
            packs = list(packs)
            for place in range(COVER):
                for at_unit, (tile, f) in enumerate(units):
                    value = cur[0, f, i * COVER + place, pl.ds(TOP + 8 * tile, 8), :]
                    packs[at_unit] = collect(place, value, packs[at_unit])
            return tuple(turn_lanes(pack, -4 * COVER) for pack in packs)

        packs = lax.fori_loop(0, LEVELS // COVER, some, (zero,) * len(units))
        for i, tile in enumerate(tiles):
            for pair in range(2):
                pack_lon(0, tile, pair, packs[4 * i + 2 * pair], packs[4 * i + 2 * pair + 1])

    loads[2].wait()
    loads[3].wait()
    cover(OUTER)
    pl.when(is_bottom)(lambda: pl.semaphore_wait(barrier, 3))
    pl.when(not_bottom)(lambda: pl.semaphore_wait(barrier, 4))
    for index in range(len(GROUPS)):
        send_up(0, index)
    loads[4].wait()
    cover(INNER)
    pack_first(INNER)
    send_lon_part(0, 0)
    pack_first(OUTER)
    send_lon_part(0, 1)
    send_lon_part(0, 2)
    for index in range(len(GROUPS)):
        send_down(0, index)

    inside, last = factors()
    for tile in range(4):
        count = wet_count[tile]
        for level in range(LEVELS):
            pivot[level, pl.ds(8 * tile, 8), :] = jnp.where(
                count > level + 1, inside[level], jnp.where(count == level + 1, last[level], 0.0)
            )

    source = lax.broadcasted_iota(jnp.int32, (COLS, COLS), 0)
    offset = lax.rem(source - lax.broadcasted_iota(jnp.int32, (COLS, COLS), 1) + COLS, COLS)

    def weigh(plus, minus, plus_2, minus_2):
        weights = jnp.where(offset == 1, plus, jnp.where(offset == COLS - 1, minus, 0.0))
        weights = jnp.where(offset == 2, plus_2, jnp.where(offset == COLS - 2, minus_2, weights))
        return weights.astype(jnp.bfloat16)

    for at_filter, taps in enumerate(((1.0, 1.0, 0.0, 0.0), (8.0, -8.0, -1.0, 1.0), (1.0, -1.0, 0.0, 0.0))):
        weights = weigh(*taps)
        for half in range(2):
            filters[pl.ds(COLS * half, COLS), pl.ds(COLS * at_filter, COLS)] = weights

    def grow(step, f, level, tile):
        if step == 0:
            return cur.at[1, f, level, pl.ds(TOP + 8 * tile, 8), :]
        return result.at[f, level, pl.ds(8 * tile, 8), :]

    def at(step, f, level, tile, shift=0):
        return cur[step, f, level, pl.ds(TOP + 8 * tile + shift, 8), :]

    def split(value):
        high = value.astype(jnp.bfloat16)
        low = (value - high.astype(jnp.float32)).astype(jnp.bfloat16)
        return jnp.concatenate([high, low], axis=1)

    def along(step, tiles):
        flat = (8 * X_LEVELS, COLS)
        for tile in tiles:
            rows = pl.ds(TOP + 8 * tile, 8)
            turned = jnp.broadcast_to(coriolis(tile)[None], (X_LEVELS, 8, COLS)).reshape(flat)

            def some(i, total):
                levels = pl.ds(i * X_LEVELS, X_LEVELS)
                value = [cur[step, f, levels, rows, :].reshape(flat) for f in range(FIELDS)]
                mixed = jnp.dot(
                    jnp.concatenate([split(v) for v in value], axis=0),
                    filters[:, : 2 * COLS],
                    preferred_element_type=jnp.float32,
                )
                half = jnp.dot(
                    split(0.02 * value[1] - 0.005 * value[0]),
                    filters[:, 2 * COLS :],
                    preferred_element_type=jnp.float32,
                )
                middles = []
                for place in range(X_LEVELS):
                    part = half[8 * place : 8 * place + 8]
                    middles.append(total + part)
                    total = middles[-1] + part
                speed = value[2] * (1.0 / 60.0)
                for f in range(FIELDS):
                    both = mixed[flat[0] * f : flat[0] * (f + 1)]
                    grown = (1.6 * value[f] + 0.1 * both[:, :COLS]) - speed * both[:, COLS:]
                    if f == 2:
                        grown = grown + (turned * value[3] - jnp.concatenate(middles, axis=0))
                    if f == 3:
                        grown = grown - turned * value[2]
                    grown = grown.reshape(X_LEVELS, 8, COLS)
                    if step == 0:
                        cur[1, f, levels, rows, :] = grown
                    else:
                        result[f, levels, pl.ds(8 * tile, 8), :] = grown
                return total

            lax.fori_loop(0, LEVELS // X_LEVELS, some, zero)

    def repair(step, tiles):
        at_126, at_127, at_0 = quarter == 0, quarter == 1, quarter == 2
        at_edge = (lane < 2) | (lane >= COLS - 2)
        for tile in tiles:
            speed = own[step, 2, tile] * (1.0 / 60.0)
            gap = [halo[f, tile] - own[step, f, tile] for f in range(FIELDS)]
            change = []
            for f in range(FIELDS):
                back_1, on_1 = pltpu.roll(gap[f], COLS - 1, 1), pltpu.roll(gap[f], 1, 1)
                back_2, on_2 = pltpu.roll(gap[f], COLS - 2, 1), pltpu.roll(gap[f], 2, 1)
                near = jnp.where(at_127, back_1, jnp.where(at_0, on_1, 0.0))
                far = jnp.where(
                    at_126,
                    -back_2,
                    jnp.where(at_127, 8.0 * back_1 - back_2, jnp.where(at_0, on_2 - 8.0 * on_1, on_2)),
                )
                change.append(0.1 * near - speed * far)
            dense = 0.02 * gap[1] - 0.005 * gap[0]
            half = jnp.where(
                at_127, pltpu.roll(dense, COLS - 1, 1), jnp.where(at_0, -pltpu.roll(dense, 1, 1), 0.0)
            )
            total = half
            for shift in (4, 8, 16, 32, 64):
                total = total + jnp.where(lane >= shift, pltpu.roll(total, shift, 1), 0.0)
            change[2] = change[2] - (2.0 * total - half)
            for f in range(FIELDS):
                for level in range(LEVELS):
                    edges[f, level, pl.ds(8 * tile, 8), :] = jnp.where(
                        at_edge, turn_lanes(change[f], 126 - 4 * level), 0.0
                    )

    def sweep(step, tiles, fields, unroll):
        units = [(tile, f) for tile in tiles for f in fields]
        forces = [tile for tile in tiles if 3 in fields]

        def one(level, parts_done, sums):
            for tile in tiles:
                sides = {}

                def beside(f):
                    if f not in sides:
                        sides[f] = at(step, f, level, tile, 1), at(step, f, level, tile, -1)
                    return sides[f]

                speed = at(step, 3, level, tile) * (1.0 / 60.0)
                speed_8 = 8.0 * speed
                to_plus, to_minus = 0.1 - speed_8, 0.1 + speed_8
                pivots = pivot[level, pl.ds(8 * tile, 8), :]
                for f in fields:
                    plus, minus = beside(f)
                    gap = at(step, f, level, tile, 2) - at(step, f, level, tile, -2)
                    total = (plus * to_plus + minus * to_minus) + gap * speed
                    if f == 3:
                        plus_t, minus_t = beside(0)
                        plus_s, minus_s = beside(1)
                        half = 0.02 * (plus_s - minus_s) - 0.005 * (plus_t - minus_t)
                        middle = sums[tile] + half
                        sums[tile] = middle + half
                        total = total - middle
                    ref = grow(step, f, level, tile)
                    known = ref[...] + edges[f, level, pl.ds(8 * tile, 8), :]
                    total = pivots * ((total + known) + parts_done[tile, f])
                    parts_done[tile, f] = total
                    ref[...] = total

        def some(i, carry):
            parts_done = dict(zip(units, carry[0]))
            sums = dict(zip(forces, carry[1]))
            for place in range(unroll):
                one(i * unroll + place, parts_done, sums)
            return tuple(parts_done[u] for u in units), tuple(sums[k] for k in forces)

        repeat(LEVELS // unroll, some, ((zero,) * len(units), (zero,) * len(forces)))

    def substitute(step, tiles, fields, unroll):
        units = [(tile, f) for tile in tiles for f in fields]
        trips = LEVELS // unroll

        def some(i, carry):
            values, packs = list(carry[0]), [turn_lanes(pack, 4 * unroll) for pack in carry[1]]
            for place in reversed(range(unroll)):
                level = (trips - 1 - i) * unroll + place
                for at_unit, (tile, f) in enumerate(units):
                    ref = grow(step, f, level, tile)
                    value = ref[...] + pivot[level, pl.ds(8 * tile, 8), :] * values[at_unit]
                    ref[...] = value
                    values[at_unit] = value
                    if step == 0:
                        packs[at_unit] = collect(place, value, packs[at_unit])
            return tuple(values), tuple(packs)

        start = ((zero,) * len(units), (zero,) * (len(units) if step == 0 else 0))
        return dict(zip(units, repeat(trips, some, start)[1]))

    every = tuple(range(FIELDS))

    def pack_next(tiles, packs):
        for tile in tiles:
            for pair in range(2):
                pack_lon(1, tile, pair, packs[tile, 2 * pair], packs[tile, 2 * pair + 1])

    def outer(step, tile, wait, send):
        packs = {}
        for index, group in enumerate(GROUPS):
            wait(step, index)
            sweep(step, (tile,), group, Y_UNROLL)
            packs.update(substitute(step, (tile,), group, 16))
            if step == 0:
                send(1, index)
        if step == 0:
            pack_next((tile,), packs)
            send_lon_part(1, 1 if tile == 0 else 2)

    along(0, OUTER)
    along(0, INNER)
    for part in range(3):
        wait_lon(0, part)
    repair(0, INNER)
    sweep(0, INNER, every, 4)
    pack_next(INNER, substitute(0, INNER, every, 8))
    send_lon_part(1, 0)
    repair(0, OUTER)
    along(1, INNER)
    outer(0, 0, wait_below, send_down)
    outer(0, 3, wait_above, send_up)

    wait_lon(1, 0)
    repair(1, INNER)
    sweep(1, INNER, every, 4)
    substitute(1, INNER, every, 8)
    along(1, OUTER)
    wait_lon(1, 1)
    wait_lon(1, 2)
    repair(1, OUTER)
    outer(1, 0, wait_below, None)
    outer(1, 3, wait_above, None)

    for step in range(2):
        for index in range(len(GROUPS)):
            up, _, down = lat_copies(step, index)
            up.wait_send()
            pl.when(not_bottom)(lambda: down.wait_send())
        for part in range(3):
            for copy in lon_copies(step, part):
                copy.wait_send()


def per_device(lons, lats, state, land_mask, wet_levels):
    any_spec = pl.BlockSpec(memory_space=pl.ANY)
    groups = len(GROUPS)
    return pl.pallas_call(
        functools.partial(kernel, lons, lats),
        out_shape=jax.ShapeDtypeStruct(state.shape, jnp.float32),
        in_specs=[pl.BlockSpec(memory_space=pltpu.HBM)] * 3,
        out_specs=pl.BlockSpec(memory_space=pltpu.VMEM),
        scratch_shapes=[
            pltpu.VMEM((2, FIELDS, LEVELS, DEPTH, COLS), jnp.float32),
            pltpu.VMEM((LEVELS, ROWS, COLS), jnp.float32),
            pltpu.VMEM((2, ROWS, COLS), jnp.int32),
            pltpu.VMEM((2, 2, 4, 2, 8, COLS), jnp.float32),
            pltpu.VMEM((2, 2, 4, 2, 8, COLS), jnp.float32),
            pltpu.VMEM((FIELDS, 4, 8, COLS), jnp.float32),
            pltpu.VMEM((FIELDS, LEVELS, ROWS, COLS), jnp.float32),
            pltpu.VMEM((2, FIELDS, 4, 8, COLS), jnp.float32),
            pltpu.VMEM((2 * COLS, 3 * COLS), jnp.bfloat16),
            pltpu.SemaphoreType.DMA((5,)),
            pltpu.SemaphoreType.DMA((2, 2, groups)),
            pltpu.SemaphoreType.DMA((2, 2, groups)),
            pltpu.SemaphoreType.DMA((2, 2, 3)),
            pltpu.SemaphoreType.DMA((2, 2, 3)),
        ],
        compiler_params=pltpu.CompilerParams(collective_id=0, has_side_effects=True, vmem_limit_bytes=24 * 2**20),
        name="ocean_steps",
    )(*(pltpu.with_memory_space_constraint(x, pltpu.HBM) for x in (state, land_mask, wet_levels)))


def solution(mesh):
    placed = (P(None, None, "lat", "lon"), P("lat", "lon"), P("lat", "lon"))
    return jax.shard_map(
        functools.partial(per_device, mesh.shape["lon"], mesh.shape["lat"]),
        mesh=mesh,
        in_specs=placed,
        out_specs=P(None, None, "lat", "lon"),
        check_vma=False,
    )
```

```python
import functools

import jax
import jax.numpy as jnp
from jax import lax
from jax.experimental import pallas as pl
from jax.experimental.pallas import tpu as pltpu
from jax.sharding import PartitionSpec as P

MESH = pl.DeviceIdType.MESH
FIELDS, LEVELS, ROWS, COLS = 4, 32, 32, 128
TOP = 8
DEPTH = 48
GROUPS = ((0, 1), (2, 3))
INNER, OUTER = (1, 2), (0, 3)
SLOT = {1: 0, 2: 1, 0: 2, 3: 3}
COVER = 8
X_LEVELS, Y_UNROLL = 32, 8


def repeat(count, body, carry):
    return body(0, carry) if count == 1 else lax.fori_loop(0, count, body, carry)


def factors():
    inside, last, ratio = [], [], 0.0
    for level in range(LEVELS):
        low = 0.5 if level > 0 else 0.0
        inside.append(0.5 / (1.5 + low + low * ratio))
        last.append(0.5 / (1.0 + low + low * ratio))
        ratio = -0.5 / (1.5 + low + low * ratio)
    return inside, last


def turn_lanes(value, amount):
    amount = amount % COLS
    return value if amount == 0 else pltpu.roll(value, amount, 1)


def column_work(at, grow, pivot, edges, collect):
    zero = jnp.zeros((8, COLS), jnp.float32)

    def sweep(step, tiles, fields, unroll):
        units = [(tile, f) for tile in tiles for f in fields]
        forces = [tile for tile in tiles if 3 in fields]

        def one(level, parts_done, sums):
            for tile in tiles:
                sides = {}

                def beside(f):
                    if f not in sides:
                        sides[f] = at(step, f, level, tile, 1), at(step, f, level, tile, -1)
                    return sides[f]

                speed = at(step, 3, level, tile) * (1.0 / 60.0)
                speed_8 = 8.0 * speed
                to_plus, to_minus = 0.1 - speed_8, 0.1 + speed_8
                pivots = pivot[level, pl.ds(8 * tile, 8), :]
                for f in fields:
                    plus, minus = beside(f)
                    gap = at(step, f, level, tile, 2) - at(step, f, level, tile, -2)
                    total = (plus * to_plus + minus * to_minus) + gap * speed
                    if f == 3:
                        plus_t, minus_t = beside(0)
                        plus_s, minus_s = beside(1)
                        half = 0.02 * (plus_s - minus_s) - 0.005 * (plus_t - minus_t)
                        middle = sums[tile] + half
                        sums[tile] = middle + half
                        total = total - middle
                    source, target = grow(step, f, level, tile)
                    known = source[...] + edges[f, level, pl.ds(8 * tile, 8), :]
                    total = pivots * ((total + known) + parts_done[tile, f])
                    parts_done[tile, f] = total
                    target[...] = total

        def some(i, carry):
            parts_done = dict(zip(units, carry[0]))
            sums = dict(zip(forces, carry[1]))
            for place in range(unroll):
                one(i * unroll + place, parts_done, sums)
            return tuple(parts_done[u] for u in units), tuple(sums[k] for k in forces)

        repeat(LEVELS // unroll, some, ((zero,) * len(units), (zero,) * len(forces)))

    def substitute(step, tiles, fields, unroll):
        units = [(tile, f) for tile in tiles for f in fields]
        trips = LEVELS // unroll

        def some(i, carry):
            values, packs = list(carry[0]), [turn_lanes(pack, 4 * unroll) for pack in carry[1]]
            for place in reversed(range(unroll)):
                level = (trips - 1 - i) * unroll + place
                for at_unit, (tile, f) in enumerate(units):
                    _, ref = grow(step, f, level, tile)
                    value = ref[...] + pivot[level, pl.ds(8 * tile, 8), :] * values[at_unit]
                    ref[...] = value
                    values[at_unit] = value
                    if step == 0:
                        packs[at_unit] = collect(place, value, packs[at_unit])
            return tuple(values), tuple(packs)

        start = ((zero,) * len(units), (zero,) * (len(units) if step == 0 else 0))
        return dict(zip(units, repeat(trips, some, start)[1]))

    return sweep, substitute


def kernel(
    lons, lats, state_ref, land_ref, depth_ref, result, cur, pivot, edges,
    mask, send_lon, recv_lon, halo, own, filters,
    load_sem, lat_send, lat_recv, lon_send, lon_recv,
):
    lon, lat = lax.axis_index("lon"), lax.axis_index("lat")
    west = {"lon": lax.rem(lon + lons - 1, lons)}
    east = {"lon": lax.rem(lon + 1, lons)}
    north, south = {"lat": lat + 1}, {"lat": lat - 1}
    fold = {"lon": lons - 1 - lon}
    is_top, is_bottom = lat == lats - 1, lat == 0
    not_top, not_bottom = lat < lats - 1, lat > 0

    barrier = pltpu.get_barrier_semaphore()

    def greet(device):
        pl.semaphore_signal(barrier, inc=1, device_id=device, device_id_type=MESH)

    greet(west)
    greet(east)
    pl.when(not_top)(lambda: greet(north))
    pl.when(is_top)(lambda: greet(fold))
    pl.when(not_bottom)(lambda: greet(south))

    loads = [
        pltpu.make_async_copy(land_ref, mask.at[0], load_sem.at[3]),
        pltpu.make_async_copy(depth_ref, mask.at[1], load_sem.at[4]),
    ] + [
        pltpu.make_async_copy(
            state_ref.at[:, :, pl.ds(8 * first, 8 * count)],
            cur.at[0, :, :, pl.ds(TOP + 8 * first, 8 * count)],
            load_sem.at[at_load],
        )
        for at_load, (first, count) in enumerate(((0, 1), (3, 1), (1, 2)))
    ]
    for load in loads:
        load.start()

    lane = lax.broadcasted_iota(jnp.int32, (8, COLS), 1)
    sublane = lax.broadcasted_iota(jnp.int32, (8, COLS), 0)
    quarter = lax.rem(lane, 4)
    low_pair = quarter < 2
    group_lane = lane // 4

    def coriolis(tile):
        row = (lat * ROWS + tile * 8 + sublane).astype(jnp.float32)
        return 0.2 * (0.2 + 0.8 * ((row + 0.5) / (lats * ROWS)))

    @pl.when(is_bottom)
    def _():
        def clear(i, carry):
            for step in range(2):
                for f in range(FIELDS):
                    cur[step, f, i, pl.ds(TOP - 2, 2), :] = jnp.zeros((2, COLS), jnp.float32)
            return carry

        lax.fori_loop(0, LEVELS, clear, 0)

    def lat_copies(step, index):
        group = GROUPS[index]
        fields = pl.ds(group[0], len(group))

        def rows(start):
            return cur.at[step, fields, :, pl.ds(start, 2)]

        up = (rows(TOP + ROWS - 2), rows(TOP - 2))
        down = (rows(TOP), rows(TOP + ROWS))
        across = (rows(TOP + ROWS - 2), rows(TOP + ROWS))

        def remote(pair, send_sem, recv_sem, device):
            return pltpu.make_async_remote_copy(
                src_ref=pair[0],
                dst_ref=pair[1],
                send_sem=send_sem.at[step, index],
                recv_sem=recv_sem.at[step, index],
                device_id=device,
                device_id_type=MESH,
            )

        return (
            remote(up, lat_send.at[0], lat_recv.at[0], north),
            remote(across, lat_send.at[0], lat_recv.at[1], fold),
            remote(down, lat_send.at[1], lat_recv.at[1], south),
        )

    def send_up(step, index):
        up, across, _ = lat_copies(step, index)
        pl.when(not_top)(lambda: up.start())
        pl.when(is_top)(lambda: across.start())

    def send_down(step, index):
        down = lat_copies(step, index)[2]
        pl.when(not_bottom)(lambda: down.start())

    def wait_below(step, index):
        up = lat_copies(step, index)[0]
        pl.when(not_bottom)(lambda: up.wait_recv())

    def wait_above(step, index):
        lat_copies(step, index)[2].wait_recv()

        @pl.when(is_top)
        def _():
            reverse = (COLS - 1) - lane
            flat = cur.reshape(2, FIELDS, LEVELS * DEPTH, COLS)
            for f in GROUPS[index]:
                for first in range(0, LEVELS, 8):
                    places = [pl.ds(first * DEPTH + TOP + ROWS + m, 8, stride=DEPTH) for m in range(2)]
                    got = [flat[step, f, place, :] for place in places]
                    got = [jnp.take_along_axis(value, reverse, axis=1) for value in got]
                    if f >= 2:
                        got = [-value for value in got]
                    flat[step, f, places[0], :] = got[1]
                    flat[step, f, places[1], :] = got[0]

    parts = ((pl.ds(0, 2), INNER), (pl.ds(2, 1), (0,)), (pl.ds(3, 1), (3,)))

    def lon_copies(step, part):
        slots = parts[part][0]

        def remote(side, device):
            return pltpu.make_async_remote_copy(
                src_ref=send_lon.at[step, side, slots],
                dst_ref=recv_lon.at[step, side, slots],
                send_sem=lon_send.at[step, side, part],
                recv_sem=lon_recv.at[step, side, part],
                device_id=device,
                device_id_type=MESH,
            )

        return remote(0, east), remote(1, west)

    def pack_lon(step, tile, pair, first, second):
        slot = SLOT[tile]
        own[step, 2 * pair, tile] = first
        own[step, 2 * pair + 1, tile] = second
        send_lon[step, 0, slot, pair] = jnp.where(low_pair, first, pltpu.roll(second, 2, 1))
        send_lon[step, 1, slot, pair] = jnp.where(low_pair, pltpu.roll(first, COLS - 2, 1), second)

    def send_lon_part(step, part):
        for copy in lon_copies(step, part):
            copy.start()

    def wait_lon(step, part):
        for copy in lon_copies(step, part):
            copy.wait_recv()
        for tile in parts[part][1]:
            for pair in range(2):
                from_west = recv_lon[step, 0, SLOT[tile], pair]
                from_east = recv_lon[step, 1, SLOT[tile], pair]
                halo[2 * pair, tile] = jnp.where(low_pair, from_west, pltpu.roll(from_east, 2, 1))
                halo[2 * pair + 1, tile] = jnp.where(
                    low_pair, pltpu.roll(from_west, COLS - 2, 1), from_east
                )

    def collect(place, value, packed):
        return jnp.where(group_lane == place, pltpu.roll(value, 4 * place + 2, 1), packed)

    zero = jnp.zeros((8, COLS), jnp.float32)

    loads[0].wait()
    loads[1].wait()
    wet_count = [
        jnp.where(mask[0, pl.ds(8 * tile, 8), :] == 1, mask[1, pl.ds(8 * tile, 8), :], 0)
        for tile in range(4)
    ]

    def cover(tiles):
        def some(i, carry):
            for place in range(COVER):
                level = i * COVER + place
                for tile in tiles:
                    wet = wet_count[tile] > level
                    for f in range(FIELDS):
                        rows = pl.ds(TOP + 8 * tile, 8)
                        cur[0, f, level, rows, :] = jnp.where(wet, cur[0, f, level, rows, :], 0.0)
            return carry

        lax.fori_loop(0, LEVELS // COVER, some, 0)

    def pack_first(tiles):
        units = [(tile, f) for tile in tiles for f in range(FIELDS)]

        def some(i, packs):
            packs = list(packs)
            for place in range(COVER):
                for at_unit, (tile, f) in enumerate(units):
                    value = cur[0, f, i * COVER + place, pl.ds(TOP + 8 * tile, 8), :]
                    packs[at_unit] = collect(place, value, packs[at_unit])
            return tuple(turn_lanes(pack, -4 * COVER) for pack in packs)

        packs = lax.fori_loop(0, LEVELS // COVER, some, (zero,) * len(units))
        for i, tile in enumerate(tiles):
            for pair in range(2):
                pack_lon(0, tile, pair, packs[4 * i + 2 * pair], packs[4 * i + 2 * pair + 1])

    loads[2].wait()
    loads[3].wait()
    cover(OUTER)
    pl.when(is_bottom)(lambda: pl.semaphore_wait(barrier, 3))
    pl.when(not_bottom)(lambda: pl.semaphore_wait(barrier, 4))
    for index in range(len(GROUPS)):
        send_up(0, index)
    loads[4].wait()
    cover(INNER)
    pack_first(INNER)
    send_lon_part(0, 0)
    pack_first(OUTER)
    send_lon_part(0, 1)
    send_lon_part(0, 2)
    for index in range(len(GROUPS)):
        send_down(0, index)

    inside, last = factors()
    for tile in range(4):
        count = wet_count[tile]
        for level in range(LEVELS):
            pivot[level, pl.ds(8 * tile, 8), :] = jnp.where(
                count > level + 1, inside[level], jnp.where(count == level + 1, last[level], 0.0)
            )

    source = lax.broadcasted_iota(jnp.int32, (COLS, COLS), 0)
    offset = lax.rem(source - lax.broadcasted_iota(jnp.int32, (COLS, COLS), 1) + COLS, COLS)

    def weigh(plus, minus, plus_2, minus_2):
        weights = jnp.where(offset == 1, plus, jnp.where(offset == COLS - 1, minus, 0.0))
        weights = jnp.where(offset == 2, plus_2, jnp.where(offset == COLS - 2, minus_2, weights))
        return weights.astype(jnp.bfloat16)

    for at_filter, taps in enumerate(((1.0, 1.0, 0.0, 0.0), (8.0, -8.0, -1.0, 1.0), (1.0, -1.0, 0.0, 0.0))):
        weights = weigh(*taps)
        for half in range(2):
            filters[pl.ds(COLS * half, COLS), pl.ds(COLS * at_filter, COLS)] = weights

    def grow(step, f, level, tile):
        if step == 0:
            ref = cur.at[1, f, level, pl.ds(TOP + 8 * tile, 8), :]
        else:
            ref = result.at[f, level, pl.ds(8 * tile, 8), :]
        return ref, ref

    def at(step, f, level, tile, shift=0):
        return cur[step, f, level, pl.ds(TOP + 8 * tile + shift, 8), :]

    def split(value):
        high = value.astype(jnp.bfloat16)
        low = (value - high.astype(jnp.float32)).astype(jnp.bfloat16)
        return jnp.concatenate([high, low], axis=1)

    def along(step, tiles):
        flat = (8 * X_LEVELS, COLS)
        for tile in tiles:
            rows = pl.ds(TOP + 8 * tile, 8)
            turned = jnp.broadcast_to(coriolis(tile)[None], (X_LEVELS, 8, COLS)).reshape(flat)

            def some(i, total):
                levels = pl.ds(i * X_LEVELS, X_LEVELS)
                value = [cur[step, f, levels, rows, :].reshape(flat) for f in range(FIELDS)]
                mixed = jnp.dot(
                    jnp.concatenate([split(v) for v in value], axis=0),
                    filters[:, : 2 * COLS],
                    preferred_element_type=jnp.float32,
                )
                half = jnp.dot(
                    split(0.02 * value[1] - 0.005 * value[0]),
                    filters[:, 2 * COLS :],
                    preferred_element_type=jnp.float32,
                )
                middles = []
                for place in range(X_LEVELS):
                    part = half[8 * place : 8 * place + 8]
                    middles.append(total + part)
                    total = middles[-1] + part
                speed = value[2] * (1.0 / 60.0)
                for f in range(FIELDS):
                    both = mixed[flat[0] * f : flat[0] * (f + 1)]
                    grown = (1.6 * value[f] + 0.1 * both[:, :COLS]) - speed * both[:, COLS:]
                    if f == 2:
                        grown = grown + (turned * value[3] - jnp.concatenate(middles, axis=0))
                    if f == 3:
                        grown = grown - turned * value[2]
                    grown = grown.reshape(X_LEVELS, 8, COLS)
                    if step == 0:
                        cur[1, f, levels, rows, :] = grown
                    else:
                        result[f, levels, pl.ds(8 * tile, 8), :] = grown
                return total

            lax.fori_loop(0, LEVELS // X_LEVELS, some, zero)

    def repair(step, tiles):
        at_126, at_127, at_0 = quarter == 0, quarter == 1, quarter == 2
        at_edge = (lane < 2) | (lane >= COLS - 2)
        for tile in tiles:
            speed = own[step, 2, tile] * (1.0 / 60.0)
            gap = [halo[f, tile] - own[step, f, tile] for f in range(FIELDS)]
            change = []
            for f in range(FIELDS):
                back_1, on_1 = pltpu.roll(gap[f], COLS - 1, 1), pltpu.roll(gap[f], 1, 1)
                back_2, on_2 = pltpu.roll(gap[f], COLS - 2, 1), pltpu.roll(gap[f], 2, 1)
                near = jnp.where(at_127, back_1, jnp.where(at_0, on_1, 0.0))
                far = jnp.where(
                    at_126,
                    -back_2,
                    jnp.where(at_127, 8.0 * back_1 - back_2, jnp.where(at_0, on_2 - 8.0 * on_1, on_2)),
                )
                change.append(0.1 * near - speed * far)
            dense = 0.02 * gap[1] - 0.005 * gap[0]
            half = jnp.where(
                at_127, pltpu.roll(dense, COLS - 1, 1), jnp.where(at_0, -pltpu.roll(dense, 1, 1), 0.0)
            )
            total = half
            for shift in (4, 8, 16, 32, 64):
                total = total + jnp.where(lane >= shift, pltpu.roll(total, shift, 1), 0.0)
            change[2] = change[2] - (2.0 * total - half)
            for f in range(FIELDS):
                for level in range(LEVELS):
                    edges[f, level, pl.ds(8 * tile, 8), :] = jnp.where(
                        at_edge, turn_lanes(change[f], 126 - 4 * level), 0.0
                    )

    sweep, substitute = column_work(at, grow, pivot, edges, collect)
    every = tuple(range(FIELDS))

    def pack_next(tiles, packs):
        for tile in tiles:
            for pair in range(2):
                pack_lon(1, tile, pair, packs[tile, 2 * pair], packs[tile, 2 * pair + 1])

    def outer(step, tile, wait, send):
        packs = {}
        for index, group in enumerate(GROUPS):
            wait(step, index)
            sweep(step, (tile,), group, Y_UNROLL)
            packs.update(substitute(step, (tile,), group, 16))
            if step == 0:
                send(1, index)
        if step == 0:
            pack_next((tile,), packs)
            send_lon_part(1, 1 if tile == 0 else 2)

    along(0, OUTER)
    along(0, INNER)
    for part in range(3):
        wait_lon(0, part)
    repair(0, INNER)
    sweep(0, INNER, every, 4)
    pack_next(INNER, substitute(0, INNER, every, 8))
    send_lon_part(1, 0)
    repair(0, OUTER)
    along(1, INNER)
    outer(0, 0, wait_below, send_down)
    outer(0, 3, wait_above, send_up)

    wait_lon(1, 0)
    repair(1, INNER)
    sweep(1, INNER, every, 4)
    substitute(1, INNER, every, 8)
    along(1, OUTER)
    wait_lon(1, 1)
    wait_lon(1, 2)
    repair(1, OUTER)
    outer(1, 0, wait_below, None)
    for index in range(len(GROUPS)):
        wait_above(1, index)

    for step in range(2):
        for index in range(len(GROUPS)):
            up, _, down = lat_copies(step, index)
            up.wait_send()
            pl.when(not_bottom)(lambda: down.wait_send())
        for part in range(3):
            for copy in lon_copies(step, part):
                copy.wait_send()


def finish(result, cur, pivot, edges, out_ref, fresh, out_sem):
    tile = 3
    copies = [
        pltpu.make_async_copy(
            result.at[f, :, pl.ds(0, 8 * tile)], out_ref.at[f, :, pl.ds(0, 8 * tile)], out_sem.at[f]
        )
        for f in range(FIELDS)
    ]
    for copy in copies:
        copy.start()

    def at(step, f, level, tile, shift=0):
        return cur[step, f, level, pl.ds(TOP + 8 * tile + shift, 8), :]

    def grow(step, f, level, tile):
        return result.at[f, level, pl.ds(8 * tile, 8), :], fresh.at[f, level]

    sweep, substitute = column_work(at, grow, pivot, edges, None)
    for index, group in enumerate(GROUPS):
        sweep(1, (tile,), group, Y_UNROLL)
        substitute(1, (tile,), group, 16)
        fields = pl.ds(group[0], len(group))
        copy = pltpu.make_async_copy(
            fresh.at[fields], out_ref.at[fields, :, pl.ds(8 * tile, 8)], out_sem.at[FIELDS + index]
        )
        copy.start()
        copies.append(copy)
    for copy in copies:
        copy.wait()


def per_device(lons, lats, state, land_mask, wet_levels):
    groups = len(GROUPS)
    block = (FIELDS, LEVELS, ROWS, COLS)
    kept = (block, (2, FIELDS, LEVELS, DEPTH, COLS), (LEVELS, ROWS, COLS), block)
    in_vmem = pl.BlockSpec(memory_space=pltpu.VMEM)
    grown = pl.pallas_call(
        functools.partial(kernel, lons, lats),
        out_shape=[jax.ShapeDtypeStruct(shape, jnp.float32) for shape in kept],
        in_specs=[pl.BlockSpec(memory_space=pltpu.HBM)] * 3,
        out_specs=[in_vmem] * 4,
        scratch_shapes=[
            pltpu.VMEM((2, ROWS, COLS), jnp.int32),
            pltpu.VMEM((2, 2, 4, 2, 8, COLS), jnp.float32),
            pltpu.VMEM((2, 2, 4, 2, 8, COLS), jnp.float32),
            pltpu.VMEM((FIELDS, 4, 8, COLS), jnp.float32),
            pltpu.VMEM((2, FIELDS, 4, 8, COLS), jnp.float32),
            pltpu.VMEM((2 * COLS, 3 * COLS), jnp.bfloat16),
            pltpu.SemaphoreType.DMA((5,)),
            pltpu.SemaphoreType.DMA((2, 2, groups)),
            pltpu.SemaphoreType.DMA((2, 2, groups)),
            pltpu.SemaphoreType.DMA((2, 2, 3)),
            pltpu.SemaphoreType.DMA((2, 2, 3)),
        ],
        compiler_params=pltpu.CompilerParams(
            collective_id=0, has_side_effects=True, vmem_limit_bytes=24 * 2**20
        ),
        name="ocean_steps",
    )(*(pltpu.with_memory_space_constraint(x, pltpu.HBM) for x in (state, land_mask, wet_levels)))
    return pl.pallas_call(
        finish,
        out_shape=jax.ShapeDtypeStruct(block, jnp.float32),
        in_specs=[in_vmem] * 4,
        out_specs=pl.BlockSpec(memory_space=pltpu.HBM),
        scratch_shapes=[
            pltpu.VMEM((FIELDS, LEVELS, 8, COLS), jnp.float32),
            pltpu.SemaphoreType.DMA((FIELDS + groups,)),
        ],
        compiler_params=pltpu.CompilerParams(vmem_limit_bytes=8 * 2**20),
        name="last_tile",
    )(*grown)


def solution(mesh):
    placed = (P(None, None, "lat", "lon"), P("lat", "lon"), P("lat", "lon"))
    return jax.shard_map(
        functools.partial(per_device, mesh.shape["lon"], mesh.shape["lat"]),
        mesh=mesh,
        in_specs=placed,
        out_specs=P(None, None, "lat", "lon"),
        check_vma=False,
    )
```

```python
import functools

import jax
import jax.numpy as jnp
from jax import lax
from jax.experimental import pallas as pl
from jax.experimental.pallas import tpu as pltpu
from jax.sharding import PartitionSpec as P

MESH = pl.DeviceIdType.MESH
FIELDS, LEVELS, ROWS, COLS = 4, 32, 32, 128
TOP = 8
DEPTH = 48
GROUPS = ((0, 1, 2, 3),)
INNER, OUTER = (1, 2), (0, 3)
SLOT = {1: 0, 2: 1, 0: 2, 3: 3}
COVER = 8
X_LEVELS, Y_UNROLL = 32, 8


def repeat(count, body, carry):
    return body(0, carry) if count == 1 else lax.fori_loop(0, count, body, carry)


def factors():
    inside, last, ratio = [], [], 0.0
    for level in range(LEVELS):
        low = 0.5 if level > 0 else 0.0
        inside.append(0.5 / (1.5 + low + low * ratio))
        last.append(0.5 / (1.0 + low + low * ratio))
        ratio = -0.5 / (1.5 + low + low * ratio)
    return inside, last


def turn_lanes(value, amount):
    amount = amount % COLS
    return value if amount == 0 else pltpu.roll(value, amount, 1)


def column_work(at, grow, pivot, edges, collect):
    zero = jnp.zeros((8, COLS), jnp.float32)

    def sweep(step, tiles, fields, unroll):
        units = [(tile, f) for tile in tiles for f in fields]
        forces = [tile for tile in tiles if 3 in fields]

        def one(level, parts_done, sums):
            for tile in tiles:
                sides = {}

                def beside(f):
                    if f not in sides:
                        sides[f] = at(step, f, level, tile, 1), at(step, f, level, tile, -1)
                    return sides[f]

                speed = at(step, 3, level, tile) * (1.0 / 60.0)
                speed_8 = 8.0 * speed
                to_plus, to_minus = 0.1 - speed_8, 0.1 + speed_8
                pivots = pivot[level, pl.ds(8 * tile, 8), :]
                for f in fields:
                    plus, minus = beside(f)
                    gap = at(step, f, level, tile, 2) - at(step, f, level, tile, -2)
                    total = (plus * to_plus + minus * to_minus) + gap * speed
                    if f == 3:
                        plus_t, minus_t = beside(0)
                        plus_s, minus_s = beside(1)
                        half = 0.02 * (plus_s - minus_s) - 0.005 * (plus_t - minus_t)
                        middle = sums[tile] + half
                        sums[tile] = middle + half
                        total = total - middle
                    source, target = grow(step, f, level, tile)
                    known = source[...] + edges[f, level, pl.ds(8 * tile, 8), :]
                    total = pivots * ((total + known) + parts_done[tile, f])
                    parts_done[tile, f] = total
                    target[...] = total

        def some(i, carry):
            parts_done = dict(zip(units, carry[0]))
            sums = dict(zip(forces, carry[1]))
            for place in range(unroll):
                one(i * unroll + place, parts_done, sums)
            return tuple(parts_done[u] for u in units), tuple(sums[k] for k in forces)

        repeat(LEVELS // unroll, some, ((zero,) * len(units), (zero,) * len(forces)))

    def substitute(step, tiles, fields, unroll):
        units = [(tile, f) for tile in tiles for f in fields]
        trips = LEVELS // unroll

        def some(i, carry):
            values, packs = list(carry[0]), [turn_lanes(pack, 4 * unroll) for pack in carry[1]]
            for place in reversed(range(unroll)):
                level = (trips - 1 - i) * unroll + place
                for at_unit, (tile, f) in enumerate(units):
                    _, ref = grow(step, f, level, tile)
                    value = ref[...] + pivot[level, pl.ds(8 * tile, 8), :] * values[at_unit]
                    ref[...] = value
                    values[at_unit] = value
                    if step == 0:
                        packs[at_unit] = collect(place, value, packs[at_unit])
            return tuple(values), tuple(packs)

        start = ((zero,) * len(units), (zero,) * (len(units) if step == 0 else 0))
        return dict(zip(units, repeat(trips, some, start)[1]))

    return sweep, substitute


def kernel(
    lons, lats, state_ref, land_ref, depth_ref, result, cur, pivot, edges,
    mask, send_lon, recv_lon, halo, own, filters,
    load_sem, lat_send, lat_recv, lon_send, lon_recv,
):
    lon, lat = lax.axis_index("lon"), lax.axis_index("lat")
    west = {"lon": lax.rem(lon + lons - 1, lons)}
    east = {"lon": lax.rem(lon + 1, lons)}
    north, south = {"lat": lat + 1}, {"lat": lat - 1}
    fold = {"lon": lons - 1 - lon}
    is_top, is_bottom = lat == lats - 1, lat == 0
    not_top, not_bottom = lat < lats - 1, lat > 0

    barrier = pltpu.get_barrier_semaphore()

    def greet(device):
        pl.semaphore_signal(barrier, inc=1, device_id=device, device_id_type=MESH)

    greet(west)
    greet(east)
    pl.when(not_top)(lambda: greet(north))
    pl.when(is_top)(lambda: greet(fold))
    pl.when(not_bottom)(lambda: greet(south))

    loads = [
        pltpu.make_async_copy(land_ref, mask.at[0], load_sem.at[3]),
        pltpu.make_async_copy(depth_ref, mask.at[1], load_sem.at[4]),
    ] + [
        pltpu.make_async_copy(
            state_ref.at[:, :, pl.ds(8 * first, 8 * count)],
            cur.at[0, :, :, pl.ds(TOP + 8 * first, 8 * count)],
            load_sem.at[at_load],
        )
        for at_load, (first, count) in enumerate(((0, 1), (3, 1), (1, 2)))
    ]
    for load in loads:
        load.start()

    lane = lax.broadcasted_iota(jnp.int32, (8, COLS), 1)
    sublane = lax.broadcasted_iota(jnp.int32, (8, COLS), 0)
    quarter = lax.rem(lane, 4)
    low_pair = quarter < 2
    group_lane = lane // 4

    def coriolis(tile):
        row = (lat * ROWS + tile * 8 + sublane).astype(jnp.float32)
        return 0.2 * (0.2 + 0.8 * ((row + 0.5) / (lats * ROWS)))

    @pl.when(is_bottom)
    def _():
        def clear(i, carry):
            for step in range(2):
                for f in range(FIELDS):
                    cur[step, f, i, pl.ds(TOP - 2, 2), :] = jnp.zeros((2, COLS), jnp.float32)
            return carry

        lax.fori_loop(0, LEVELS, clear, 0)

    def lat_copies(step, index):
        group = GROUPS[index]
        fields = pl.ds(group[0], len(group))

        def rows(start):
            return cur.at[step, fields, :, pl.ds(start, 2)]

        up = (rows(TOP + ROWS - 2), rows(TOP - 2))
        down = (rows(TOP), rows(TOP + ROWS))
        across = (rows(TOP + ROWS - 2), rows(TOP + ROWS))

        def remote(pair, send_sem, recv_sem, device):
            return pltpu.make_async_remote_copy(
                src_ref=pair[0],
                dst_ref=pair[1],
                send_sem=send_sem.at[step, index],
                recv_sem=recv_sem.at[step, index],
                device_id=device,
                device_id_type=MESH,
            )

        return (
            remote(up, lat_send.at[0], lat_recv.at[0], north),
            remote(across, lat_send.at[0], lat_recv.at[1], fold),
            remote(down, lat_send.at[1], lat_recv.at[1], south),
        )

    def send_up(step, index):
        up, across, _ = lat_copies(step, index)
        pl.when(not_top)(lambda: up.start())
        pl.when(is_top)(lambda: across.start())

    def send_down(step, index):
        down = lat_copies(step, index)[2]
        pl.when(not_bottom)(lambda: down.start())

    def wait_below(step, index):
        up = lat_copies(step, index)[0]
        pl.when(not_bottom)(lambda: up.wait_recv())

    def wait_above(step, index):
        lat_copies(step, index)[2].wait_recv()

        @pl.when(is_top)
        def _():
            reverse = (COLS - 1) - lane
            flat = cur.reshape(2, FIELDS, LEVELS * DEPTH, COLS)
            for f in GROUPS[index]:
                for first in range(0, LEVELS, 8):
                    places = [pl.ds(first * DEPTH + TOP + ROWS + m, 8, stride=DEPTH) for m in range(2)]
                    got = [flat[step, f, place, :] for place in places]
                    got = [jnp.take_along_axis(value, reverse, axis=1) for value in got]
                    if f >= 2:
                        got = [-value for value in got]
                    flat[step, f, places[0], :] = got[1]
                    flat[step, f, places[1], :] = got[0]

    parts = ((pl.ds(0, 2), INNER), (pl.ds(2, 1), (0,)), (pl.ds(3, 1), (3,)))

    def lon_copies(step, part):
        slots = parts[part][0]

        def remote(side, device):
            return pltpu.make_async_remote_copy(
                src_ref=send_lon.at[step, side, slots],
                dst_ref=recv_lon.at[step, side, slots],
                send_sem=lon_send.at[step, side, part],
                recv_sem=lon_recv.at[step, side, part],
                device_id=device,
                device_id_type=MESH,
            )

        return remote(0, east), remote(1, west)

    def pack_lon(step, tile, pair, first, second):
        slot = SLOT[tile]
        own[step, 2 * pair, tile] = first
        own[step, 2 * pair + 1, tile] = second
        send_lon[step, 0, slot, pair] = jnp.where(low_pair, first, pltpu.roll(second, 2, 1))
        send_lon[step, 1, slot, pair] = jnp.where(low_pair, pltpu.roll(first, COLS - 2, 1), second)

    def send_lon_part(step, part):
        for copy in lon_copies(step, part):
            copy.start()

    def wait_lon(step, part):
        for copy in lon_copies(step, part):
            copy.wait_recv()
        for tile in parts[part][1]:
            for pair in range(2):
                from_west = recv_lon[step, 0, SLOT[tile], pair]
                from_east = recv_lon[step, 1, SLOT[tile], pair]
                halo[2 * pair, tile] = jnp.where(low_pair, from_west, pltpu.roll(from_east, 2, 1))
                halo[2 * pair + 1, tile] = jnp.where(
                    low_pair, pltpu.roll(from_west, COLS - 2, 1), from_east
                )

    def collect(place, value, packed):
        return jnp.where(group_lane == place, pltpu.roll(value, 4 * place + 2, 1), packed)

    zero = jnp.zeros((8, COLS), jnp.float32)

    loads[0].wait()
    loads[1].wait()
    wet_count = [
        jnp.where(mask[0, pl.ds(8 * tile, 8), :] == 1, mask[1, pl.ds(8 * tile, 8), :], 0)
        for tile in range(4)
    ]

    def cover(tiles):
        def some(i, carry):
            for place in range(COVER):
                level = i * COVER + place
                for tile in tiles:
                    wet = wet_count[tile] > level
                    for f in range(FIELDS):
                        rows = pl.ds(TOP + 8 * tile, 8)
                        cur[0, f, level, rows, :] = jnp.where(wet, cur[0, f, level, rows, :], 0.0)
            return carry

        lax.fori_loop(0, LEVELS // COVER, some, 0)

    def pack_first(tiles):
        units = [(tile, f) for tile in tiles for f in range(FIELDS)]

        def some(i, packs):
            packs = list(packs)
            for place in range(COVER):
                for at_unit, (tile, f) in enumerate(units):
                    value = cur[0, f, i * COVER + place, pl.ds(TOP + 8 * tile, 8), :]
                    packs[at_unit] = collect(place, value, packs[at_unit])
            return tuple(turn_lanes(pack, -4 * COVER) for pack in packs)

        packs = lax.fori_loop(0, LEVELS // COVER, some, (zero,) * len(units))
        for i, tile in enumerate(tiles):
            for pair in range(2):
                pack_lon(0, tile, pair, packs[4 * i + 2 * pair], packs[4 * i + 2 * pair + 1])

    loads[2].wait()
    loads[3].wait()
    cover(OUTER)
    pl.when(is_bottom)(lambda: pl.semaphore_wait(barrier, 3))
    pl.when(not_bottom)(lambda: pl.semaphore_wait(barrier, 4))
    for index in range(len(GROUPS)):
        send_up(0, index)
    loads[4].wait()
    cover(INNER)
    pack_first(INNER)
    send_lon_part(0, 0)
    pack_first(OUTER)
    send_lon_part(0, 1)
    send_lon_part(0, 2)
    for index in range(len(GROUPS)):
        send_down(0, index)

    inside, last = factors()
    for tile in range(4):
        count = wet_count[tile]
        for level in range(LEVELS):
            pivot[level, pl.ds(8 * tile, 8), :] = jnp.where(
                count > level + 1, inside[level], jnp.where(count == level + 1, last[level], 0.0)
            )

    source = lax.broadcasted_iota(jnp.int32, (COLS, COLS), 0)
    offset = lax.rem(source - lax.broadcasted_iota(jnp.int32, (COLS, COLS), 1) + COLS, COLS)

    def weigh(plus, minus, plus_2, minus_2):
        weights = jnp.where(offset == 1, plus, jnp.where(offset == COLS - 1, minus, 0.0))
        weights = jnp.where(offset == 2, plus_2, jnp.where(offset == COLS - 2, minus_2, weights))
        return weights.astype(jnp.bfloat16)

    for at_filter, taps in enumerate(((1.0, 1.0, 0.0, 0.0), (8.0, -8.0, -1.0, 1.0), (1.0, -1.0, 0.0, 0.0))):
        weights = weigh(*taps)
        for half in range(2):
            filters[pl.ds(COLS * half, COLS), pl.ds(COLS * at_filter, COLS)] = weights

    def grow(step, f, level, tile):
        if step == 0:
            ref = cur.at[1, f, level, pl.ds(TOP + 8 * tile, 8), :]
        else:
            ref = result.at[f, level, pl.ds(8 * tile, 8), :]
        return ref, ref

    def at(step, f, level, tile, shift=0):
        return cur[step, f, level, pl.ds(TOP + 8 * tile + shift, 8), :]

    def split(value):
        high = value.astype(jnp.bfloat16)
        low = (value - high.astype(jnp.float32)).astype(jnp.bfloat16)
        return jnp.concatenate([high, low], axis=1)

    def along(step, tiles):
        flat = (8 * X_LEVELS, COLS)
        for tile in tiles:
            rows = pl.ds(TOP + 8 * tile, 8)
            turned = jnp.broadcast_to(coriolis(tile)[None], (X_LEVELS, 8, COLS)).reshape(flat)

            def some(i, total):
                levels = pl.ds(i * X_LEVELS, X_LEVELS)
                value = [cur[step, f, levels, rows, :].reshape(flat) for f in range(FIELDS)]
                mixed = jnp.dot(
                    jnp.concatenate([split(v) for v in value], axis=0),
                    filters[:, : 2 * COLS],
                    preferred_element_type=jnp.float32,
                )
                half = jnp.dot(
                    split(0.02 * value[1] - 0.005 * value[0]),
                    filters[:, 2 * COLS :],
                    preferred_element_type=jnp.float32,
                )
                middles = []
                for place in range(X_LEVELS):
                    part = half[8 * place : 8 * place + 8]
                    middles.append(total + part)
                    total = middles[-1] + part
                speed = value[2] * (1.0 / 60.0)
                for f in range(FIELDS):
                    both = mixed[flat[0] * f : flat[0] * (f + 1)]
                    grown = (1.6 * value[f] + 0.1 * both[:, :COLS]) - speed * both[:, COLS:]
                    if f == 2:
                        grown = grown + (turned * value[3] - jnp.concatenate(middles, axis=0))
                    if f == 3:
                        grown = grown - turned * value[2]
                    grown = grown.reshape(X_LEVELS, 8, COLS)
                    if step == 0:
                        cur[1, f, levels, rows, :] = grown
                    else:
                        result[f, levels, pl.ds(8 * tile, 8), :] = grown
                return total

            lax.fori_loop(0, LEVELS // X_LEVELS, some, zero)

    def repair(step, tiles):
        at_126, at_127, at_0 = quarter == 0, quarter == 1, quarter == 2
        at_edge = (lane < 2) | (lane >= COLS - 2)
        for tile in tiles:
            speed = own[step, 2, tile] * (1.0 / 60.0)
            gap = [halo[f, tile] - own[step, f, tile] for f in range(FIELDS)]
            change = []
            for f in range(FIELDS):
                back_1, on_1 = pltpu.roll(gap[f], COLS - 1, 1), pltpu.roll(gap[f], 1, 1)
                back_2, on_2 = pltpu.roll(gap[f], COLS - 2, 1), pltpu.roll(gap[f], 2, 1)
                near = jnp.where(at_127, back_1, jnp.where(at_0, on_1, 0.0))
                far = jnp.where(
                    at_126,
                    -back_2,
                    jnp.where(at_127, 8.0 * back_1 - back_2, jnp.where(at_0, on_2 - 8.0 * on_1, on_2)),
                )
                change.append(0.1 * near - speed * far)
            dense = 0.02 * gap[1] - 0.005 * gap[0]
            half = jnp.where(
                at_127, pltpu.roll(dense, COLS - 1, 1), jnp.where(at_0, -pltpu.roll(dense, 1, 1), 0.0)
            )
            total = half
            for shift in (4, 8, 16, 32, 64):
                total = total + jnp.where(lane >= shift, pltpu.roll(total, shift, 1), 0.0)
            change[2] = change[2] - (2.0 * total - half)
            for f in range(FIELDS):
                for level in range(LEVELS):
                    edges[f, level, pl.ds(8 * tile, 8), :] = jnp.where(
                        at_edge, turn_lanes(change[f], 126 - 4 * level), 0.0
                    )

    sweep, substitute = column_work(at, grow, pivot, edges, collect)
    every = tuple(range(FIELDS))

    def pack_next(tiles, packs):
        for tile in tiles:
            for pair in range(2):
                pack_lon(1, tile, pair, packs[tile, 2 * pair], packs[tile, 2 * pair + 1])

    def outer(step, tile, wait, send):
        packs = {}
        for index, group in enumerate(GROUPS):
            wait(step, index)
            sweep(step, (tile,), group, Y_UNROLL)
            packs.update(substitute(step, (tile,), group, 16))
            if step == 0:
                send(1, index)
        if step == 0:
            pack_next((tile,), packs)
            send_lon_part(1, 1 if tile == 0 else 2)

    along(0, OUTER)
    along(0, INNER)
    for part in range(3):
        wait_lon(0, part)
    repair(0, INNER)
    sweep(0, INNER, every, 4)
    pack_next(INNER, substitute(0, INNER, every, 8))
    send_lon_part(1, 0)
    repair(0, OUTER)
    along(1, INNER)
    outer(0, 0, wait_below, send_down)
    outer(0, 3, wait_above, send_up)

    wait_lon(1, 0)
    repair(1, INNER)
    sweep(1, INNER, every, 4)
    substitute(1, INNER, every, 8)
    along(1, OUTER)
    wait_lon(1, 1)
    wait_lon(1, 2)
    repair(1, OUTER)
    outer(1, 0, wait_below, None)
    for index in range(len(GROUPS)):
        wait_above(1, index)

    for step in range(2):
        for index in range(len(GROUPS)):
            up, _, down = lat_copies(step, index)
            up.wait_send()
            pl.when(not_bottom)(lambda: down.wait_send())
        for part in range(3):
            for copy in lon_copies(step, part):
                copy.wait_send()


def finish(result, cur, pivot, edges, out_ref, fresh, out_sem):
    tile = 3
    copies = [
        pltpu.make_async_copy(
            result.at[f, :, pl.ds(0, 8 * tile)], out_ref.at[f, :, pl.ds(0, 8 * tile)], out_sem.at[f]
        )
        for f in range(FIELDS)
    ]
    for copy in copies:
        copy.start()

    def at(step, f, level, tile, shift=0):
        return cur[step, f, level, pl.ds(TOP + 8 * tile + shift, 8), :]

    def grow(step, f, level, tile):
        return result.at[f, level, pl.ds(8 * tile, 8), :], fresh.at[f, level]

    sweep, substitute = column_work(at, grow, pivot, edges, None)
    for index, group in enumerate(GROUPS):
        sweep(1, (tile,), group, Y_UNROLL)
        substitute(1, (tile,), group, 16)
        fields = pl.ds(group[0], len(group))
        copy = pltpu.make_async_copy(
            fresh.at[fields], out_ref.at[fields, :, pl.ds(8 * tile, 8)], out_sem.at[FIELDS + index]
        )
        copy.start()
        copies.append(copy)
    for copy in copies:
        copy.wait()


def per_device(lons, lats, state, land_mask, wet_levels):
    groups = len(GROUPS)
    block = (FIELDS, LEVELS, ROWS, COLS)
    kept = (block, (2, FIELDS, LEVELS, DEPTH, COLS), (LEVELS, ROWS, COLS), block)
    in_vmem = pl.BlockSpec(memory_space=pltpu.VMEM)
    grown = pl.pallas_call(
        functools.partial(kernel, lons, lats),
        out_shape=[jax.ShapeDtypeStruct(shape, jnp.float32) for shape in kept],
        in_specs=[pl.BlockSpec(memory_space=pltpu.HBM)] * 3,
        out_specs=[in_vmem] * 4,
        scratch_shapes=[
            pltpu.VMEM((2, ROWS, COLS), jnp.int32),
            pltpu.VMEM((2, 2, 4, 2, 8, COLS), jnp.float32),
            pltpu.VMEM((2, 2, 4, 2, 8, COLS), jnp.float32),
            pltpu.VMEM((FIELDS, 4, 8, COLS), jnp.float32),
            pltpu.VMEM((2, FIELDS, 4, 8, COLS), jnp.float32),
            pltpu.VMEM((2 * COLS, 3 * COLS), jnp.bfloat16),
            pltpu.SemaphoreType.DMA((5,)),
            pltpu.SemaphoreType.DMA((2, 2, groups)),
            pltpu.SemaphoreType.DMA((2, 2, groups)),
            pltpu.SemaphoreType.DMA((2, 2, 3)),
            pltpu.SemaphoreType.DMA((2, 2, 3)),
        ],
        compiler_params=pltpu.CompilerParams(
            collective_id=0, has_side_effects=True, vmem_limit_bytes=24 * 2**20
        ),
        name="ocean_steps",
    )(*(pltpu.with_memory_space_constraint(x, pltpu.HBM) for x in (state, land_mask, wet_levels)))
    return pl.pallas_call(
        finish,
        out_shape=jax.ShapeDtypeStruct(block, jnp.float32),
        in_specs=[in_vmem] * 4,
        out_specs=pl.BlockSpec(memory_space=pltpu.HBM),
        scratch_shapes=[
            pltpu.VMEM((FIELDS, LEVELS, 8, COLS), jnp.float32),
            pltpu.SemaphoreType.DMA((FIELDS + groups,)),
        ],
        compiler_params=pltpu.CompilerParams(vmem_limit_bytes=8 * 2**20),
        name="last_tile",
    )(*grown)


def solution(mesh):
    placed = (P(None, None, "lat", "lon"), P("lat", "lon"), P("lat", "lon"))
    return jax.shard_map(
        functools.partial(per_device, mesh.shape["lon"], mesh.shape["lat"]),
        mesh=mesh,
        in_specs=placed,
        out_specs=P(None, None, "lat", "lon"),
        check_vma=False,
    )
```

```python
import functools

import jax
import jax.numpy as jnp
from jax import lax
from jax.experimental import pallas as pl
from jax.experimental.pallas import tpu as pltpu
from jax.sharding import PartitionSpec as P

MESH = pl.DeviceIdType.MESH
FIELDS, LEVELS, ROWS, COLS = 4, 32, 32, 128
TOP = 8
DEPTH = 48
GROUPS = ((0, 1), (2, 3))
INNER, OUTER = (1, 2), (0, 3)
SLOT = {1: 0, 2: 1, 0: 2, 3: 3}
COVER = 8
X_LEVELS, Y_UNROLL = 32, 8


def repeat(count, body, carry):
    return body(0, carry) if count == 1 else lax.fori_loop(0, count, body, carry)


def factors():
    inside, last, ratio = [], [], 0.0
    for level in range(LEVELS):
        low = 0.5 if level > 0 else 0.0
        inside.append(0.5 / (1.5 + low + low * ratio))
        last.append(0.5 / (1.0 + low + low * ratio))
        ratio = -0.5 / (1.5 + low + low * ratio)
    return inside, last


def turn_lanes(value, amount):
    amount = amount % COLS
    return value if amount == 0 else pltpu.roll(value, amount, 1)


def column_work(at, grow, pivot, edges, collect):
    zero = jnp.zeros((8, COLS), jnp.float32)

    def sweep(step, tiles, fields, unroll):
        units = [(tile, f) for tile in tiles for f in fields]
        forces = [tile for tile in tiles if 3 in fields]

        def one(level, parts_done, sums):
            for tile in tiles:
                sides = {}

                def beside(f):
                    if f not in sides:
                        sides[f] = at(step, f, level, tile, 1), at(step, f, level, tile, -1)
                    return sides[f]

                speed = at(step, 3, level, tile) * (1.0 / 60.0)
                speed_8 = 8.0 * speed
                to_plus, to_minus = 0.1 - speed_8, 0.1 + speed_8
                pivots = pivot[level, pl.ds(8 * tile, 8), :]
                for f in fields:
                    plus, minus = beside(f)
                    gap = at(step, f, level, tile, 2) - at(step, f, level, tile, -2)
                    total = (plus * to_plus + minus * to_minus) + gap * speed
                    if f == 3:
                        plus_t, minus_t = beside(0)
                        plus_s, minus_s = beside(1)
                        half = 0.02 * (plus_s - minus_s) - 0.005 * (plus_t - minus_t)
                        middle = sums[tile] + half
                        sums[tile] = middle + half
                        total = total - middle
                    source, target = grow(step, f, level, tile)
                    known = source[...] + edges[f, level, pl.ds(8 * tile, 8), :]
                    total = pivots * ((total + known) + parts_done[tile, f])
                    parts_done[tile, f] = total
                    target[...] = total

        def some(i, carry):
            parts_done = dict(zip(units, carry[0]))
            sums = dict(zip(forces, carry[1]))
            for place in range(unroll):
                one(i * unroll + place, parts_done, sums)
            return tuple(parts_done[u] for u in units), tuple(sums[k] for k in forces)

        repeat(LEVELS // unroll, some, ((zero,) * len(units), (zero,) * len(forces)))

    def substitute(step, tiles, fields, unroll):
        units = [(tile, f) for tile in tiles for f in fields]
        trips = LEVELS // unroll

        def some(i, carry):
            values, packs = list(carry[0]), [turn_lanes(pack, 4 * unroll) for pack in carry[1]]
            for place in reversed(range(unroll)):
                level = (trips - 1 - i) * unroll + place
                for at_unit, (tile, f) in enumerate(units):
                    _, ref = grow(step, f, level, tile)
                    value = ref[...] + pivot[level, pl.ds(8 * tile, 8), :] * values[at_unit]
                    ref[...] = value
                    values[at_unit] = value
                    if step == 0:
                        packs[at_unit] = collect(place, value, packs[at_unit])
            return tuple(values), tuple(packs)

        start = ((zero,) * len(units), (zero,) * (len(units) if step == 0 else 0))
        return dict(zip(units, repeat(trips, some, start)[1]))

    return sweep, substitute


def kernel(
    lons, lats, state_ref, land_ref, depth_ref, result, cur, pivot, edges,
    mask, send_lon, recv_lon, halo, own, filters,
    load_sem, lat_send, lat_recv, lon_send, lon_recv,
):
    lon, lat = lax.axis_index("lon"), lax.axis_index("lat")
    west = {"lon": lax.rem(lon + lons - 1, lons)}
    east = {"lon": lax.rem(lon + 1, lons)}
    north, south = {"lat": lat + 1}, {"lat": lat - 1}
    fold = {"lon": lons - 1 - lon}
    is_top, is_bottom = lat == lats - 1, lat == 0
    not_top, not_bottom = lat < lats - 1, lat > 0

    barrier = pltpu.get_barrier_semaphore()

    def greet(device):
        pl.semaphore_signal(barrier, inc=1, device_id=device, device_id_type=MESH)

    greet(west)
    greet(east)
    pl.when(not_top)(lambda: greet(north))
    pl.when(is_top)(lambda: greet(fold))
    pl.when(not_bottom)(lambda: greet(south))

    loads = [
        pltpu.make_async_copy(land_ref, mask.at[0], load_sem.at[3]),
        pltpu.make_async_copy(depth_ref, mask.at[1], load_sem.at[4]),
    ] + [
        pltpu.make_async_copy(
            state_ref.at[:, :, pl.ds(8 * first, 8 * count)],
            cur.at[0, :, :, pl.ds(TOP + 8 * first, 8 * count)],
            load_sem.at[at_load],
        )
        for at_load, (first, count) in enumerate(((0, 1), (3, 1), (1, 2)))
    ]
    for load in loads:
        load.start()

    lane = lax.broadcasted_iota(jnp.int32, (8, COLS), 1)
    sublane = lax.broadcasted_iota(jnp.int32, (8, COLS), 0)
    quarter = lax.rem(lane, 4)
    low_pair = quarter < 2
    group_lane = lane // 4

    def coriolis(tile):
        row = (lat * ROWS + tile * 8 + sublane).astype(jnp.float32)
        return 0.2 * (0.2 + 0.8 * ((row + 0.5) / (lats * ROWS)))

    @pl.when(is_bottom)
    def _():
        def clear(i, carry):
            for step in range(2):
                for f in range(FIELDS):
                    cur[step, f, i, pl.ds(TOP - 2, 2), :] = jnp.zeros((2, COLS), jnp.float32)
            return carry

        lax.fori_loop(0, LEVELS, clear, 0)

    def lat_copies(step, index):
        group = GROUPS[index]
        fields = pl.ds(group[0], len(group))

        def rows(start):
            return cur.at[step, fields, :, pl.ds(start, 2)]

        up = (rows(TOP + ROWS - 2), rows(TOP - 2))
        down = (rows(TOP), rows(TOP + ROWS))
        across = (rows(TOP + ROWS - 2), rows(TOP + ROWS))

        def remote(pair, send_sem, recv_sem, device):
            return pltpu.make_async_remote_copy(
                src_ref=pair[0],
                dst_ref=pair[1],
                send_sem=send_sem.at[step, index],
                recv_sem=recv_sem.at[step, index],
                device_id=device,
                device_id_type=MESH,
            )

        return (
            remote(up, lat_send.at[0], lat_recv.at[0], north),
            remote(across, lat_send.at[0], lat_recv.at[1], fold),
            remote(down, lat_send.at[1], lat_recv.at[1], south),
        )

    def send_up(step, index):
        up, across, _ = lat_copies(step, index)
        pl.when(not_top)(lambda: up.start())
        pl.when(is_top)(lambda: across.start())

    def send_down(step, index):
        down = lat_copies(step, index)[2]
        pl.when(not_bottom)(lambda: down.start())

    def wait_below(step, index):
        up = lat_copies(step, index)[0]
        pl.when(not_bottom)(lambda: up.wait_recv())

    def wait_above(step, index):
        lat_copies(step, index)[2].wait_recv()

        @pl.when(is_top)
        def _():
            reverse = (COLS - 1) - lane
            flat = cur.reshape(2, FIELDS, LEVELS * DEPTH, COLS)
            for f in GROUPS[index]:
                for first in range(0, LEVELS, 8):
                    places = [pl.ds(first * DEPTH + TOP + ROWS + m, 8, stride=DEPTH) for m in range(2)]
                    got = [flat[step, f, place, :] for place in places]
                    got = [jnp.take_along_axis(value, reverse, axis=1) for value in got]
                    if f >= 2:
                        got = [-value for value in got]
                    flat[step, f, places[0], :] = got[1]
                    flat[step, f, places[1], :] = got[0]

    parts = ((pl.ds(0, 2), INNER), (pl.ds(2, 1), (0,)), (pl.ds(3, 1), (3,)))

    def lon_copies(step, part):
        slots = parts[part][0]

        def remote(side, device):
            return pltpu.make_async_remote_copy(
                src_ref=send_lon.at[step, side, slots],
                dst_ref=recv_lon.at[step, side, slots],
                send_sem=lon_send.at[step, side, part],
                recv_sem=lon_recv.at[step, side, part],
                device_id=device,
                device_id_type=MESH,
            )

        return remote(0, east), remote(1, west)

    def pack_lon(step, tile, pair, first, second):
        slot = SLOT[tile]
        own[step, 2 * pair, tile] = first
        own[step, 2 * pair + 1, tile] = second
        send_lon[step, 0, slot, pair] = jnp.where(low_pair, first, pltpu.roll(second, 2, 1))
        send_lon[step, 1, slot, pair] = jnp.where(low_pair, pltpu.roll(first, COLS - 2, 1), second)

    def send_lon_part(step, part):
        for copy in lon_copies(step, part):
            copy.start()

    def wait_lon(step, part):
        for copy in lon_copies(step, part):
            copy.wait_recv()
        for tile in parts[part][1]:
            for pair in range(2):
                from_west = recv_lon[step, 0, SLOT[tile], pair]
                from_east = recv_lon[step, 1, SLOT[tile], pair]
                halo[2 * pair, tile] = jnp.where(low_pair, from_west, pltpu.roll(from_east, 2, 1))
                halo[2 * pair + 1, tile] = jnp.where(
                    low_pair, pltpu.roll(from_west, COLS - 2, 1), from_east
                )

    def collect(place, value, packed):
        return jnp.where(group_lane == place, pltpu.roll(value, 4 * place + 2, 1), packed)

    zero = jnp.zeros((8, COLS), jnp.float32)

    loads[0].wait()
    loads[1].wait()
    wet_count = [
        jnp.where(mask[0, pl.ds(8 * tile, 8), :] == 1, mask[1, pl.ds(8 * tile, 8), :], 0)
        for tile in range(4)
    ]

    def cover(tiles):
        def some(i, carry):
            for place in range(COVER):
                level = i * COVER + place
                for tile in tiles:
                    wet = wet_count[tile] > level
                    for f in range(FIELDS):
                        rows = pl.ds(TOP + 8 * tile, 8)
                        cur[0, f, level, rows, :] = jnp.where(wet, cur[0, f, level, rows, :], 0.0)
            return carry

        lax.fori_loop(0, LEVELS // COVER, some, 0)

    def pack_first(tiles):
        units = [(tile, f) for tile in tiles for f in range(FIELDS)]

        def some(i, packs):
            packs = list(packs)
            for place in range(COVER):
                for at_unit, (tile, f) in enumerate(units):
                    value = cur[0, f, i * COVER + place, pl.ds(TOP + 8 * tile, 8), :]
                    packs[at_unit] = collect(place, value, packs[at_unit])
            return tuple(turn_lanes(pack, -4 * COVER) for pack in packs)

        packs = lax.fori_loop(0, LEVELS // COVER, some, (zero,) * len(units))
        for i, tile in enumerate(tiles):
            for pair in range(2):
                pack_lon(0, tile, pair, packs[4 * i + 2 * pair], packs[4 * i + 2 * pair + 1])

    loads[2].wait()
    loads[3].wait()
    cover(OUTER)
    pl.when(is_bottom)(lambda: pl.semaphore_wait(barrier, 3))
    pl.when(not_bottom)(lambda: pl.semaphore_wait(barrier, 4))
    for index in range(len(GROUPS)):
        send_up(0, index)
    loads[4].wait()
    cover(INNER)
    pack_first(INNER)
    send_lon_part(0, 0)
    pack_first(OUTER)
    send_lon_part(0, 1)
    send_lon_part(0, 2)
    for index in range(len(GROUPS)):
        send_down(0, index)

    inside, last = factors()
    for tile in range(4):
        count = wet_count[tile]
        for level in range(LEVELS):
            pivot[level, pl.ds(8 * tile, 8), :] = jnp.where(
                count > level + 1, inside[level], jnp.where(count == level + 1, last[level], 0.0)
            )

    source = lax.broadcasted_iota(jnp.int32, (COLS, COLS), 0)
    offset = lax.rem(source - lax.broadcasted_iota(jnp.int32, (COLS, COLS), 1) + COLS, COLS)

    def weigh(plus, minus, plus_2, minus_2):
        weights = jnp.where(offset == 1, plus, jnp.where(offset == COLS - 1, minus, 0.0))
        weights = jnp.where(offset == 2, plus_2, jnp.where(offset == COLS - 2, minus_2, weights))
        return weights.astype(jnp.bfloat16)

    for at_filter, taps in enumerate(((1.0, 1.0, 0.0, 0.0), (8.0, -8.0, -1.0, 1.0), (1.0, -1.0, 0.0, 0.0))):
        weights = weigh(*taps)
        for half in range(2):
            filters[pl.ds(COLS * half, COLS), pl.ds(COLS * at_filter, COLS)] = weights

    def grow(step, f, level, tile):
        if step == 0:
            ref = cur.at[1, f, level, pl.ds(TOP + 8 * tile, 8), :]
        else:
            ref = result.at[f, level, pl.ds(8 * tile, 8), :]
        return ref, ref

    def at(step, f, level, tile, shift=0):
        return cur[step, f, level, pl.ds(TOP + 8 * tile + shift, 8), :]

    def split(value):
        high = value.astype(jnp.bfloat16)
        low = (value - high.astype(jnp.float32)).astype(jnp.bfloat16)
        return jnp.concatenate([high, low], axis=1)

    def along(step, tiles):
        flat = (8 * X_LEVELS, COLS)
        for tile in tiles:
            rows = pl.ds(TOP + 8 * tile, 8)
            turned = jnp.broadcast_to(coriolis(tile)[None], (X_LEVELS, 8, COLS)).reshape(flat)

            def some(i, total):
                levels = pl.ds(i * X_LEVELS, X_LEVELS)
                value = [cur[step, f, levels, rows, :].reshape(flat) for f in range(FIELDS)]
                mixed = jnp.dot(
                    jnp.concatenate([split(v) for v in value], axis=0),
                    filters[:, : 2 * COLS],
                    preferred_element_type=jnp.float32,
                )
                half = jnp.dot(
                    split(0.02 * value[1] - 0.005 * value[0]),
                    filters[:, 2 * COLS :],
                    preferred_element_type=jnp.float32,
                )
                middles = []
                for place in range(X_LEVELS):
                    part = half[8 * place : 8 * place + 8]
                    middles.append(total + part)
                    total = middles[-1] + part
                speed = value[2] * (1.0 / 60.0)
                for f in range(FIELDS):
                    both = mixed[flat[0] * f : flat[0] * (f + 1)]
                    grown = (1.6 * value[f] + 0.1 * both[:, :COLS]) - speed * both[:, COLS:]
                    if f == 2:
                        grown = grown + (turned * value[3] - jnp.concatenate(middles, axis=0))
                    if f == 3:
                        grown = grown - turned * value[2]
                    grown = grown.reshape(X_LEVELS, 8, COLS)
                    if step == 0:
                        cur[1, f, levels, rows, :] = grown
                    else:
                        result[f, levels, pl.ds(8 * tile, 8), :] = grown
                return total

            lax.fori_loop(0, LEVELS // X_LEVELS, some, zero)

    def repair(step, tiles):
        at_126, at_127, at_0 = quarter == 0, quarter == 1, quarter == 2
        at_edge = (lane < 2) | (lane >= COLS - 2)
        for tile in tiles:
            speed = own[step, 2, tile] * (1.0 / 60.0)
            gap = [halo[f, tile] - own[step, f, tile] for f in range(FIELDS)]
            change = []
            for f in range(FIELDS):
                back_1, on_1 = pltpu.roll(gap[f], COLS - 1, 1), pltpu.roll(gap[f], 1, 1)
                back_2, on_2 = pltpu.roll(gap[f], COLS - 2, 1), pltpu.roll(gap[f], 2, 1)
                near = jnp.where(at_127, back_1, jnp.where(at_0, on_1, 0.0))
                far = jnp.where(
                    at_126,
                    -back_2,
                    jnp.where(at_127, 8.0 * back_1 - back_2, jnp.where(at_0, on_2 - 8.0 * on_1, on_2)),
                )
                change.append(0.1 * near - speed * far)
            dense = 0.02 * gap[1] - 0.005 * gap[0]
            half = jnp.where(
                at_127, pltpu.roll(dense, COLS - 1, 1), jnp.where(at_0, -pltpu.roll(dense, 1, 1), 0.0)
            )
            total = half
            for shift in (4, 8, 16, 32, 64):
                total = total + jnp.where(lane >= shift, pltpu.roll(total, shift, 1), 0.0)
            change[2] = change[2] - (2.0 * total - half)
            for f in range(FIELDS):
                for level in range(LEVELS):
                    edges[f, level, pl.ds(8 * tile, 8), :] = jnp.where(
                        at_edge, turn_lanes(change[f], 126 - 4 * level), 0.0
                    )

    sweep, substitute = column_work(at, grow, pivot, edges, collect)
    every = tuple(range(FIELDS))

    def pack_next(tiles, packs):
        for tile in tiles:
            for pair in range(2):
                pack_lon(1, tile, pair, packs[tile, 2 * pair], packs[tile, 2 * pair + 1])

    def outer(step, tile, wait, send):
        packs = {}
        for index, group in enumerate(GROUPS):
            wait(step, index)
            sweep(step, (tile,), group, Y_UNROLL)
            packs.update(substitute(step, (tile,), group, 16))
            if step == 0:
                send(1, index)
        if step == 0:
            pack_next((tile,), packs)
            send_lon_part(1, 1 if tile == 0 else 2)

    along(0, OUTER)
    along(0, INNER)
    for part in range(3):
        wait_lon(0, part)
    repair(0, INNER)
    sweep(0, INNER, every, 4)
    pack_next(INNER, substitute(0, INNER, every, 8))
    send_lon_part(1, 0)
    repair(0, OUTER)
    along(1, INNER)
    outer(0, 3, wait_above, send_up)
    outer(0, 0, wait_below, send_down)

    wait_lon(1, 0)
    repair(1, INNER)
    sweep(1, INNER, every, 4)
    substitute(1, INNER, every, 8)
    along(1, OUTER)
    wait_lon(1, 1)
    wait_lon(1, 2)
    repair(1, OUTER)
    outer(1, 0, wait_below, None)
    for index in range(len(GROUPS)):
        wait_above(1, index)

    for step in range(2):
        for index in range(len(GROUPS)):
            up, _, down = lat_copies(step, index)
            up.wait_send()
            pl.when(not_bottom)(lambda: down.wait_send())
        for part in range(3):
            for copy in lon_copies(step, part):
                copy.wait_send()


def finish(result, cur, pivot, edges, out_ref, fresh, out_sem):
    tile = 3
    copies = [
        pltpu.make_async_copy(
            result.at[f, :, pl.ds(0, 8 * tile)], out_ref.at[f, :, pl.ds(0, 8 * tile)], out_sem.at[f]
        )
        for f in range(FIELDS)
    ]
    for copy in copies:
        copy.start()

    def at(step, f, level, tile, shift=0):
        return cur[step, f, level, pl.ds(TOP + 8 * tile + shift, 8), :]

    def grow(step, f, level, tile):
        return result.at[f, level, pl.ds(8 * tile, 8), :], fresh.at[f, level]

    sweep, substitute = column_work(at, grow, pivot, edges, None)
    for index, group in enumerate(GROUPS):
        sweep(1, (tile,), group, Y_UNROLL)
        substitute(1, (tile,), group, 16)
        fields = pl.ds(group[0], len(group))
        copy = pltpu.make_async_copy(
            fresh.at[fields], out_ref.at[fields, :, pl.ds(8 * tile, 8)], out_sem.at[FIELDS + index]
        )
        copy.start()
        copies.append(copy)
    for copy in copies:
        copy.wait()


def per_device(lons, lats, state, land_mask, wet_levels):
    groups = len(GROUPS)
    block = (FIELDS, LEVELS, ROWS, COLS)
    kept = (block, (2, FIELDS, LEVELS, DEPTH, COLS), (LEVELS, ROWS, COLS), block)
    in_vmem = pl.BlockSpec(memory_space=pltpu.VMEM)
    grown = pl.pallas_call(
        functools.partial(kernel, lons, lats),
        out_shape=[jax.ShapeDtypeStruct(shape, jnp.float32) for shape in kept],
        in_specs=[pl.BlockSpec(memory_space=pltpu.HBM)] * 3,
        out_specs=[in_vmem] * 4,
        scratch_shapes=[
            pltpu.VMEM((2, ROWS, COLS), jnp.int32),
            pltpu.VMEM((2, 2, 4, 2, 8, COLS), jnp.float32),
            pltpu.VMEM((2, 2, 4, 2, 8, COLS), jnp.float32),
            pltpu.VMEM((FIELDS, 4, 8, COLS), jnp.float32),
            pltpu.VMEM((2, FIELDS, 4, 8, COLS), jnp.float32),
            pltpu.VMEM((2 * COLS, 3 * COLS), jnp.bfloat16),
            pltpu.SemaphoreType.DMA((5,)),
            pltpu.SemaphoreType.DMA((2, 2, groups)),
            pltpu.SemaphoreType.DMA((2, 2, groups)),
            pltpu.SemaphoreType.DMA((2, 2, 3)),
            pltpu.SemaphoreType.DMA((2, 2, 3)),
        ],
        compiler_params=pltpu.CompilerParams(
            collective_id=0, has_side_effects=True, vmem_limit_bytes=24 * 2**20
        ),
        name="ocean_steps",
    )(*(pltpu.with_memory_space_constraint(x, pltpu.HBM) for x in (state, land_mask, wet_levels)))
    return pl.pallas_call(
        finish,
        out_shape=jax.ShapeDtypeStruct(block, jnp.float32),
        in_specs=[in_vmem] * 4,
        out_specs=pl.BlockSpec(memory_space=pltpu.HBM),
        scratch_shapes=[
            pltpu.VMEM((FIELDS, LEVELS, 8, COLS), jnp.float32),
            pltpu.SemaphoreType.DMA((FIELDS + groups,)),
        ],
        compiler_params=pltpu.CompilerParams(vmem_limit_bytes=8 * 2**20),
        name="last_tile",
    )(*grown)


def solution(mesh):
    placed = (P(None, None, "lat", "lon"), P("lat", "lon"), P("lat", "lon"))
    return jax.shard_map(
        functools.partial(per_device, mesh.shape["lon"], mesh.shape["lat"]),
        mesh=mesh,
        in_specs=placed,
        out_specs=P(None, None, "lat", "lon"),
        check_vma=False,
    )
```
